32 devices in a mesh: grp: 2 (over y), ctx: 4 (over z), ch: 4 (over x, core).
Axes of the slice: x: 2, y: 2, z: 4, core: 2. Of those that a mesh axis runs over, the one named last changes fastest.
Arguments:
- fwd_hidden: bfloat16 [4096, 2048], P(('grp', 'ctx'), 'ch'), parts along dimension 0, may hold values from -6 to 6
- rev_hidden: bfloat16 [4096, 2048], P(('grp', 'ctx'), 'ch'), parts along dimension 0, may hold values from -6 to 6
- bases: int32 [4096], P(('grp', 'ctx')), parts along dimension 0, may hold values from 0 to 3
- complement: int32 [4], replicated, may hold values from 0 to 3, each once
- offsets: int32 [32], P('grp'), parts along dimension 0, may hold values from 0 to 2047, as said below
- base_embed: bfloat16 [4, 2048], P(None, 'ch'), may hold values from -6 to 6
- norm_gain: float32 [2048], replicated, may hold values from 0.1 to 1.9
- in_weight: bfloat16 [4, 2048, 2048], P(None, 'ctx', 'ch'), may hold values from -0.125 to 0.125
- filters: float32 [3, 16, 128], P(None, 'ch'), may hold values from -0.5 to 0.5
- out_weight: bfloat16 [2048, 2048], P('ctx', 'ch'), may hold values from -0.125 to 0.125
Outputs:
- block_out: bfloat16 [4096, 2048], P(('grp', 'ctx'), 'ch'), parts along dimension 0
The draws below stay inside these ranges and needn't reach their ends.
There are 2 independent parts, one for each index of `grp`. The reference program is written for one: setup_inputs(seed, part) draws one part's arguments, and reference() takes and returns one part's arrays. A program takes and returns all parts, laid end to end along the dimension named above; an argument that names none is the same for every part. Nothing has to cross between parts.
Inputs may be any that keep to these rules, and one draw needn't show every extreme that they name: The first offset is 0, the last is 2047, and the offsets rise strictly; each is the first position of a document. `complement`: A permutation of the 4 letters.
All inputs are finite; a program needn't handle non-finite values.
Results may differ from the reference program's by a relative error of at most 0.012.
Values may be sent and summed in bfloat16 or wider, within the bound.
No kernel may reach another device: no remote copies, remote signals or barrier semaphores. Data moves between devices by JAX's collectives and lax.ppermute only.
A program may use at most 64 MiB of HBM per device.

```python
import jax
import jax.numpy as jnp
import numpy as np
from jax import lax

D = 2048
HEADS = 16
TAPS = 128
SECTIONS = 3
NB = 4
NDOC = 16
SEQ = 2048


def draw_offsets(key, part):
    picks = jax.random.permutation(key, SEQ - 2)[:NDOC - 2] + 1
    starts = jnp.sort(picks.astype(jnp.int32))
    first = jnp.zeros((1,), jnp.int32)
    final = jnp.full((1,), SEQ - 1, jnp.int32)
    return jnp.concatenate([first, starts, final]).astype(jnp.int32)


def with_ends(values, own_key, least, largest):
    longest = values.shape.index(max(values.shape))
    spots = []
    for shift in (0, 1):
        where = [jax.random.randint(jax.random.fold_in(own_key, axis), (), 0, length) for axis, length in enumerate(values.shape)]
        where[longest] = (where[longest] + shift) % values.shape[longest]
        spots.append(tuple(where))
    return values.at[spots[0]].set(least).at[spots[1]].set(largest)


def level_of(stream_key, shape, split, least, top_value):
    def one(axis_at, shards_of):
        steps = jax.random.uniform(jax.random.fold_in(jax.random.fold_in(stream_key, 6), axis_at), (shards_of,), jnp.float32, least / len(split), top_value / len(split))
        return jnp.repeat(jnp.exp(steps), shape[axis_at] // shards_of).reshape((-1,) + (1,) * (len(shape) - axis_at - 1))

    loudness = one(*split[0])
    for cut in split[1:]:
        loudness = loudness * one(*cut)
    return loudness


def gaussian(stream_key, shape, spread, limit, split=(), held_as=jnp.bfloat16):
    entries = spread * jax.random.normal(stream_key, shape, jnp.float32)
    if split:
        entries = entries * level_of(stream_key, shape, split, -0.22, 0.18)
    return jnp.clip(entries, -limit, limit).astype(held_as)


def setup_inputs(seed: int = 0, part: int = 0) -> dict:
    streams_of = jax.random.split(jax.random.key(seed), 11)
    part_keys = jax.random.split(jax.random.fold_in(streams_of[10], part), 11)
    fwd_hidden = gaussian(part_keys[0], (SEQ, D), 1.0, 6.0, ((0, 4), (1, 4)))
    rev_hidden = gaussian(part_keys[1], (SEQ, D), 1.0, 6.0, ((0, 4), (1, 4)))
    bases = with_ends(jax.random.randint(part_keys[2], (SEQ,), 0, NB), jax.random.fold_in(part_keys[2], 1), 0, NB - 1).astype(jnp.int32)
    complement = jax.random.permutation(streams_of[3], NB).astype(jnp.int32)
    offsets = draw_offsets(jax.random.fold_in(jax.random.fold_in(streams_of[10], part), 71), part)
    base_embed = gaussian(streams_of[5], (NB, D), 1.0, 6.0, ((1, 4),))
    norm_gain = jnp.clip(1.0 + 0.18 * jax.random.normal(streams_of[6], (D,), jnp.float32), 0.1, 1.9)
    in_weight = gaussian(streams_of[7], (SECTIONS + 1, D, D), D ** -0.5, 0.125, ((1, 4), (2, 4)))
    filters = gaussian(streams_of[8], (SECTIONS, HEADS, TAPS), TAPS ** -0.5, 0.5, ((1, 4),), jnp.float32)
    out_weight = gaussian(streams_of[9], (D, D), D ** -0.5, 0.125, ((0, 4), (1, 4)))
    return {"fwd_hidden": fwd_hidden, "rev_hidden": rev_hidden, "bases": bases, "complement": complement, "offsets": offsets, "base_embed": base_embed, "norm_gain": norm_gain, "in_weight": in_weight, "filters": filters, "out_weight": out_weight}


def doc_of(positions, offsets, seq_len):
    count = lax.optimization_barrier(jnp.sum((offsets[None, :] <= positions[:, None]).astype(jnp.int32), axis=1)) - 1
    inside = (positions >= 0) & (positions < seq_len)
    return jnp.where(inside, count, -1).astype(jnp.int32)

def toeplitz(taps, backward):
    block = taps.shape[-1]
    rows_t = np.arange(block)[:, None]
    cols_s = np.arange(2 * block)[None, :]
    lag = cols_s - rows_t if backward else rows_t + block - cols_s
    valid = (lag >= 0) & (lag < block)
    index = np.clip(lag, 0, block - 1)
    return jnp.where(valid[None], taps[:, index], 0).astype(taps.dtype)

def rms_norm(values, gain):
    floats = values.astype(jnp.float32)
    scale = lax.rsqrt(lax.optimization_barrier(jnp.mean(floats * floats, axis=-1, keepdims=True)) + 1e-05)
    return (floats * scale * gain).astype(jnp.bfloat16)

def conv_ref(conv_in, taps, docs, backward):
    seq_len, width = conv_in.shape
    heads, block = taps.shape
    head_dim = width // heads
    blocks = seq_len // block
    pad_rows = jnp.zeros((block, width), jnp.float32)
    pad_docs = jnp.full((block,), -1, jnp.int32)
    if backward:
        extended = jnp.concatenate([conv_in, pad_rows], axis=0)
        ext_docs = jnp.concatenate([docs, pad_docs], axis=0)
    else:
        extended = jnp.concatenate([pad_rows, conv_in], axis=0)
        ext_docs = jnp.concatenate([pad_docs, docs], axis=0)
    table = toeplitz(taps, backward)
    shift_target = 0 if backward else block

    def one_block(number):
        start = (number * block).astype(jnp.int32)
        window = lax.dynamic_slice_in_dim(extended, start, 2 * block, 0).reshape(2 * block, heads, head_dim)
        window_docs = lax.dynamic_slice_in_dim(ext_docs, start, 2 * block, 0)
        target_docs = lax.dynamic_slice_in_dim(ext_docs, (start + shift_target).astype(jnp.int32), block, 0)
        mask = (target_docs[:, None] == window_docs[None, :]).astype(jnp.float32)
        kernel = table * mask[None]
        return jnp.einsum('hts,shd->thd', kernel, window)
    result = lax.map(one_block, jnp.arange(blocks, dtype=jnp.int32))
    return result.reshape(seq_len, width)

def strand(normed, in_weight, taps, docs, backward):
    proj = [jnp.dot(normed, in_weight[b], preferred_element_type=jnp.float32) for b in range(in_weight.shape[0])]
    state = proj[0]
    for section in range(taps.shape[0]):
        conv_in = lax.optimization_barrier(state.astype(jnp.bfloat16)).astype(jnp.float32)
        state = proj[section + 1] * conv_ref(conv_in, taps[section], docs, backward)
    return state.astype(jnp.bfloat16)

def reference(fwd_hidden, rev_hidden, bases, complement, offsets, base_embed, norm_gain, in_weight, filters, out_weight):
    seq_len = fwd_hidden.shape[0]
    positions = jnp.arange(seq_len, dtype=jnp.int32)
    docs = doc_of(positions, offsets, seq_len)
    table = base_embed.astype(jnp.float32)
    fwd_input = (fwd_hidden.astype(jnp.float32) + table[bases]).astype(jnp.bfloat16)
    rev_input = (rev_hidden.astype(jnp.float32) + table[complement[bases]]).astype(jnp.bfloat16)
    taps = lax.optimization_barrier(filters.astype(jnp.bfloat16)).astype(jnp.float32)
    fwd_mixed = strand(rms_norm(fwd_input, norm_gain), in_weight, taps, docs, False)
    rev_mixed = strand(rms_norm(rev_input, norm_gain), in_weight, taps, docs, True)
    mixed_sum = (fwd_mixed.astype(jnp.float32) + rev_mixed.astype(jnp.float32)).astype(jnp.bfloat16)
    total = jnp.dot(mixed_sum, out_weight, preferred_element_type=jnp.float32)
    return total.astype(jnp.bfloat16)
```

```python
import functools

import jax
import jax.numpy as jnp
from jax import lax
from jax.experimental import pallas as pl
from jax.experimental.pallas import tpu as pltpu
from jax.sharding import PartitionSpec as P

VMEM_LIMIT = 40 * 1024 * 1024


def partner(block, axis, apart):
    count = lax.axis_size(axis)
    route = []
    for low in range(count):
        high = low | 1 << apart
        if high != low and high < count:
            route += [(low, high), (high, low)]
    return lax.ppermute(block, axis, route)


def shifted(value, axis, by):
    count = lax.axis_size(axis)
    pairs = [(i, i + by) for i in range(count) if 0 <= i + by < count]
    return lax.ppermute(value, axis, pairs)


def doc_of(positions, offsets, seq_len):
    count = jnp.sum((offsets[None, :] <= positions[:, None]).astype(jnp.int32), axis=1) - 1
    inside = (positions >= 0) & (positions < seq_len)
    return jnp.where(inside, count, -1)


def toeplitz(taps):
    heads, block = taps.shape
    pattern = jnp.concatenate(
        [jnp.zeros((heads, 1), taps.dtype), taps[:, ::-1], jnp.zeros((heads, block), taps.dtype)],
        axis=1,
    )
    repeated = jnp.tile(pattern, (1, block))
    return repeated[:, : block * 2 * block].reshape(heads, block, 2 * block)


def rms_norm(values, gain):
    floats = values.astype(jnp.float32)
    scale = lax.rsqrt(jnp.mean(floats * floats, axis=-1, keepdims=True) + 1e-05)
    return (floats * scale * gain).astype(jnp.bfloat16)


def blockwise_conv(conv_in, rim, taps, ext_docs):
    rows, width = conv_in.shape
    heads, block = taps.shape
    head_dim = width // heads
    blocks = rows // block
    extended = jnp.concatenate([rim, conv_in], axis=0)
    target_docs = ext_docs[block:].reshape(blocks, block)
    window = jnp.concatenate(
        [
            extended[:rows].reshape(blocks, block, width),
            extended[block:].reshape(blocks, block, width),
        ],
        axis=1,
    )
    window = window.reshape(blocks, 2 * block, heads, head_dim)
    window_docs = jnp.concatenate(
        [ext_docs[:rows].reshape(blocks, block), ext_docs[block:].reshape(blocks, block)], axis=1
    )
    mask = (target_docs[:, :, None] == window_docs[:, None, :]).astype(jnp.bfloat16)
    kernel = toeplitz(taps)[None] * mask[:, None]
    result = jnp.einsum("nhts,nshd->nthd", kernel, window, preferred_element_type=jnp.float32)
    return result.reshape(rows, width)


def local(
    fwd_hidden,
    rev_hidden,
    bases,
    complement,
    offsets,
    base_embed,
    norm_gain,
    in_weight,
    filters,
    out_weight,
):
    rows, width_local = fwd_hidden.shape
    ctx_count = lax.axis_size("ctx")
    here = lax.axis_index("ctx")
    seq_len = rows * ctx_count
    letters = base_embed.shape[0]
    alphabet = jnp.arange(letters, dtype=jnp.int32)
    onehot = (bases[:, None] == alphabet[None, :]).astype(jnp.bfloat16)
    swap_table = (complement[:, None] == alphabet[None, :]).astype(jnp.bfloat16)
    onehot_rev = jnp.dot(onehot, swap_table, preferred_element_type=jnp.float32).astype(
        jnp.bfloat16
    )
    embed_fwd = jnp.dot(onehot, base_embed, preferred_element_type=jnp.float32)
    embed_rev = jnp.dot(onehot_rev, base_embed, preferred_element_type=jnp.float32)
    fwd_input = (fwd_hidden.astype(jnp.float32) + embed_fwd).astype(jnp.bfloat16)
    rev_input = (rev_hidden.astype(jnp.float32) + embed_rev).astype(jnp.bfloat16)
    levels = ctx_count.bit_length() - 1
    for level in range(levels):
        rev_input = partner(rev_input, "ctx", level)
    rev_input = rev_input[::-1]
    full_fwd, full_rev = (
        lax.all_gather(fwd_input, "ch", axis=1, tiled=True),
        lax.all_gather(rev_input, "ch", axis=1, tiled=True),
    )
    normed_fwd = rms_norm(full_fwd, norm_gain)
    normed_rev = rms_norm(full_rev, norm_gain)
    piece = lax.all_gather(in_weight, "ctx", axis=1, tiled=True)
    add_fwd = jnp.einsum("rd,bdc->brc", normed_fwd, piece, preferred_element_type=jnp.float32)
    add_rev = jnp.einsum("rd,bdc->brc", normed_rev, piece, preferred_element_type=jnp.float32)
    taps_all = filters.astype(jnp.bfloat16)
    block = filters.shape[-1]
    before = here * rows - block + jnp.arange(rows + block, dtype=jnp.int32)
    docs_fwd = doc_of(before, offsets, seq_len)
    docs_rev = doc_of(seq_len - 1 - before, offsets, seq_len)
    state_fwd = add_fwd[0]
    state_rev = add_rev[0]
    for section in range(filters.shape[0]):
        in_fwd = state_fwd.astype(jnp.bfloat16)
        in_rev = state_rev.astype(jnp.bfloat16)
        rim_fwd, rim_rev = shifted((in_fwd[-block:], in_rev[-block:]), "ctx", 1)
        conv_rev = blockwise_conv(in_rev, rim_rev, taps_all[section], docs_rev)
        conv_fwd = blockwise_conv(in_fwd, rim_fwd, taps_all[section], docs_fwd)
        state_fwd = add_fwd[section + 1] * conv_fwd
        state_rev = add_rev[section + 1] * conv_rev
    mixed_fwd = state_fwd.astype(jnp.bfloat16)
    mixed_rev = state_rev.astype(jnp.bfloat16)
    for level in range(levels):
        mixed_rev = partner(mixed_rev, "ctx", level)
    mixed_rev = mixed_rev[::-1]
    mixed_sum = (mixed_fwd.astype(jnp.float32) + mixed_rev.astype(jnp.float32)).astype(jnp.bfloat16)
    whole_sum = lax.all_gather(mixed_sum, "ch", axis=1, tiled=True)
    total = jnp.dot(
        whole_sum,
        lax.all_gather(out_weight, "ctx", axis=0, tiled=True),
        preferred_element_type=jnp.float32,
    )
    return total.astype(jnp.bfloat16)


def flip(block, axis, bit):
    count = lax.axis_size(axis)
    return lax.ppermute(block, axis, [(i, i ^ bit) for i in range(count)])


def across(block, bit):
    groups, count = lax.axis_size("grp"), lax.axis_size("ch")
    pairs = [
        (g * count + k, (g ^ 1) * count + (k ^ bit)) for g in range(groups) for k in range(count)
    ]
    return lax.ppermute(block, ("grp", "ch"), pairs)


def params(*semantics):
    return pltpu.CompilerParams(
        dimension_semantics=semantics, vmem_limit_bytes=VMEM_LIMIT
    )


def norm_kernel(place, gain, *refs):
    pieces, out = refs[:-1], refs[-1]
    strands, groups, rows, model = out.shape
    width = pieces[0].shape[-1]
    parts = model // width
    for s in range(strands):
        for g in range(groups):
            group = pieces[(s * groups + g) * parts : (s * groups + g + 1) * parts]
            floats = [p[...].astype(jnp.float32) for p in group]
            total = sum(jnp.sum(f * f, axis=-1, keepdims=True) for f in floats)
            scale = lax.rsqrt(total / model + 1e-05)
            for j, f in enumerate(floats):
                at = pl.multiple_of((place[0] ^ j) * width, width)
                lanes = pl.ds(at, width)
                out[s, g, :, lanes] = (f * scale * gain[:, lanes]).astype(jnp.bfloat16)


def norm_all(place, gain, pieces, rows, width, parts):
    flat = [p for strand in pieces for group in strand for p in group]
    strands, groups = len(pieces), len(pieces[0])
    tile = 128
    return pl.pallas_call(
        norm_kernel,
        grid_spec=pltpu.PrefetchScalarGridSpec(
            num_scalar_prefetch=1,
            grid=(rows // tile,),
            in_specs=[pl.BlockSpec((1, width * parts), lambda i, p: (0, 0))]
            + [pl.BlockSpec((tile, width), lambda i, p: (i, 0)) for _ in flat],
            out_specs=pl.BlockSpec(
                (strands, groups, tile, width * parts), lambda i, p: (0, 0, i, 0)
            ),
        ),
        out_shape=jax.ShapeDtypeStruct((strands, groups, rows, width * parts), jnp.bfloat16),
        compiler_params=params("arbitrary"),
        cost_estimate=pl.CostEstimate(
            flops=6 * strands * groups * rows * width * parts,
            bytes_accessed=4 * strands * groups * rows * width * parts,
            transcendentals=0,
        ),
        name="norm",
    )(place, gain.reshape(1, -1), *flat)


def project(normed, weight, b):
    count, _, depth, _ = weight.shape
    parts = [
        jnp.dot(
            normed[:, z * depth : (z + 1) * depth],
            weight[z, b],
            preferred_element_type=jnp.float32,
        )
        for z in range(count)
    ]
    return sum(parts[1:], parts[0])


def keep_rims(value, s, g, rim_fwd, rim_rev):
    rows, block = value.shape[0], rim_fwd.shape[1]

    @pl.when(s == 0)
    def _():
        rim_fwd[g] = value[rows - block :]

    @pl.when(s == 1)
    def _():
        rim_rev[g] = value[:block]


def first_kernel(normed, weight, state, rim_fwd, rim_rev):
    s, g = pl.program_id(0), pl.program_id(1)
    value = project(normed[0, 0], weight, 0).astype(jnp.bfloat16)
    state[0, 0] = value
    keep_rims(value, s, g, rim_fwd, rim_rev)


def first(normed, weight, block):
    strands, groups, rows, model = normed.shape
    count, few, depth, width = weight.shape
    rim = jax.ShapeDtypeStruct((groups, block, width), jnp.bfloat16)
    rim_spec = pl.BlockSpec((groups, block, width), lambda s, g: (0, 0, 0))
    return pl.pallas_call(
        first_kernel,
        grid=(strands, groups),
        in_specs=[
            pl.BlockSpec((1, 1, rows, model), lambda s, g: (s, g, 0, 0)),
            pl.BlockSpec((count, 1, depth, width), lambda s, g: (0, 0, 0, 0)),
        ],
        out_specs=[
            pl.BlockSpec((1, 1, rows, width), lambda s, g: (s, g, 0, 0)),
            rim_spec,
            rim_spec,
        ],
        out_shape=[
            jax.ShapeDtypeStruct((strands, groups, rows, width), jnp.bfloat16),
            rim,
            rim,
        ],
        compiler_params=params("arbitrary", "arbitrary"),
        cost_estimate=pl.CostEstimate(
            flops=2 * strands * groups * rows * model * width,
            bytes_accessed=2 * strands * groups * rows * model + 2 * model * width,
            transcendentals=0,
        ),
        name="first",
    )(normed, weight)


def gates_kernel(normed, weight, *outs):
    for i, out in enumerate(outs):
        out[0, 0] = project(normed[0, 0], weight, 1 + i)


def gates(normed, weight):
    strands, groups, rows, model = normed.shape
    count, few, depth, width = weight.shape
    tile = rows // 2
    shape = jax.ShapeDtypeStruct((strands, groups, rows, width), jnp.float32)
    return pl.pallas_call(
        gates_kernel,
        grid=(strands, groups, rows // tile),
        in_specs=[
            pl.BlockSpec((1, 1, tile, model), lambda s, g, i: (s, g, i, 0)),
            pl.BlockSpec((count, few, depth, width), lambda s, g, i: (0, 0, 0, 0)),
        ],
        out_specs=[pl.BlockSpec((1, 1, tile, width), lambda s, g, i: (s, g, i, 0))] * (few - 1),
        out_shape=[shape] * (few - 1),
        compiler_params=params("arbitrary", "arbitrary", "arbitrary"),
        cost_estimate=pl.CostEstimate(
            flops=2 * (few - 1) * strands * groups * rows * model * width,
            bytes_accessed=2 * strands * groups * rows * model + 2 * few * model * width,
            transcendentals=0,
        ),
        name="gates",
    )(normed, weight)


def conv_kernel(last, state, rim_fwd, rim_rev, table, mask, *refs):
    s, g = pl.program_id(0), pl.program_id(1)
    extended = refs[-1]
    rows, width = state.shape[2:]
    block = rim_fwd.shape[1]
    heads = table.shape[2]
    head = width // heads

    @pl.when(s == 0)
    def _():
        extended[:block] = rim_fwd[g]
        extended[block:] = state[0, 0]

    @pl.when(s == 1)
    def _():
        extended[:rows] = state[0, 0]
        extended[rows:] = rim_rev[g]

    for n in range(rows // block):
        span = slice(n * block, (n + 1) * block)
        for h in range(heads):
            lanes = slice(h * head, (h + 1) * head)
            kernel = table[0, 0, h] * mask[0, 0, n]
            conv = jnp.dot(
                kernel,
                extended[n * block : (n + 2) * block, lanes],
                preferred_element_type=jnp.float32,
            )
            if last:
                refs[0][0, 0, span, lanes] = conv
            else:
                refs[1][0, 0, span, lanes] = (refs[0][0, 0, span, lanes] * conv).astype(
                    jnp.bfloat16
                )
    if not last:
        keep_rims(refs[1][0, 0], s, g, refs[2], refs[3])


def conv_section(state, rims, tables, mask, section, gate=None):
    strands, groups, rows, width = state.shape
    heads, block = tables.shape[2:4]
    rim = jax.ShapeDtypeStruct((groups, block, width), jnp.bfloat16)
    rim_spec = pl.BlockSpec((groups, block, width), lambda s, g: (0, 0, 0))
    row_spec = pl.BlockSpec((1, 1, rows, width), lambda s, g: (s, g, 0, 0))
    last = gate is None
    in_specs = [
        row_spec,
        rim_spec,
        rim_spec,
        pl.BlockSpec((1, 1, heads, block, 2 * block), lambda s, g: (section, s, 0, 0, 0)),
        pl.BlockSpec(
            (1, 1, rows // block, block, 2 * block), lambda s, g: (s, g, 0, 0, 0)
        ),
    ]
    args = [state, rims[0], rims[1], tables, mask]
    if last:
        out_specs = [row_spec]
        out_shape = [jax.ShapeDtypeStruct(state.shape, jnp.float32)]
    else:
        in_specs.append(row_spec)
        args.append(gate)
        out_specs = [row_spec, rim_spec, rim_spec]
        out_shape = [jax.ShapeDtypeStruct(state.shape, jnp.bfloat16), rim, rim]
    return pl.pallas_call(
        functools.partial(conv_kernel, last),
        grid=(strands, groups),
        in_specs=in_specs,
        out_specs=out_specs,
        out_shape=out_shape,
        scratch_shapes=[pltpu.VMEM((rows + block, width), jnp.bfloat16)],
        compiler_params=params("arbitrary", "arbitrary"),
        cost_estimate=pl.CostEstimate(
            flops=4 * strands * groups * rows * block * width,
            bytes_accessed=10 * strands * groups * rows * width,
            transcendentals=0,
        ),
        name="conv",
    )(*args)


def mix_kernel(normed, weight, conv, out):
    strands = normed.shape[0]
    total = None
    for s in range(strands):
        gate = project(normed[s, 0], weight, 0)
        state = (gate * conv[s, 0]).astype(jnp.bfloat16).astype(jnp.float32)
        total = state if total is None else total + state
    out[...] = total.astype(jnp.bfloat16)


def mix(normed, weight, conv, group):
    strands, groups, rows, model = normed.shape
    count, _, depth, width = weight.shape
    tile = rows // 2
    return pl.pallas_call(
        mix_kernel,
        grid=(rows // tile,),
        in_specs=[
            pl.BlockSpec((strands, 1, tile, model), lambda i: (0, group, i, 0)),
            pl.BlockSpec((count, 1, depth, width), lambda i: (0, 0, 0, 0)),
            pl.BlockSpec((strands, 1, tile, width), lambda i: (0, group, i, 0)),
        ],
        out_specs=pl.BlockSpec((tile, width), lambda i: (i, 0)),
        out_shape=jax.ShapeDtypeStruct((rows, width), jnp.bfloat16),
        compiler_params=params("arbitrary"),
        cost_estimate=pl.CostEstimate(
            flops=2 * strands * rows * model * width,
            bytes_accessed=2 * strands * rows * model + 2 * model * width,
            transcendentals=0,
        ),
        name="mix",
    )(normed, weight, conv)


def out_kernel(place, near, far, *refs):
    pieces, out = refs[:-1], refs[-1]
    half = len(pieces) // 2
    total = None
    for weight, group in ((near, pieces[:half]), (far, pieces[half:])):
        for j, piece in enumerate(group):
            term = jnp.dot(piece[...], weight[place[0] ^ j], preferred_element_type=jnp.float32)
            total = term if total is None else total + term
    out[...] = total.astype(jnp.bfloat16)


def project_out(place, near, far, pieces):
    rows, width = pieces[0].shape
    whole = pl.BlockSpec(near.shape, lambda i, p: (0, 0, 0))
    tile = rows // 2
    return pl.pallas_call(
        out_kernel,
        grid_spec=pltpu.PrefetchScalarGridSpec(
            num_scalar_prefetch=1,
            grid=(rows // tile,),
            in_specs=[whole, whole]
            + [pl.BlockSpec((tile, width), lambda i, p: (i, 0)) for _ in pieces],
            out_specs=pl.BlockSpec((tile, near.shape[-1]), lambda i, p: (i, 0)),
        ),
        out_shape=jax.ShapeDtypeStruct((rows, near.shape[-1]), jnp.bfloat16),
        compiler_params=params("arbitrary"),
        cost_estimate=pl.CostEstimate(
            flops=2 * rows * width * len(pieces) * near.shape[-1],
            bytes_accessed=2 * near.size * 2 + 2 * rows * width * len(pieces),
            transcendentals=0,
        ),
        name="out",
    )(place, near, far, *pieces)


def conv_tables(taps):
    sections, heads, block = taps.shape
    zero = jnp.zeros((sections, heads, block), taps.dtype)
    one = jnp.zeros((sections, heads, 1), taps.dtype)
    patterns = jnp.stack(
        [
            jnp.concatenate([one, taps[:, :, ::-1], zero], axis=-1),
            jnp.concatenate([taps, zero, one], axis=-1),
        ],
        axis=1,
    )
    repeated = jnp.tile(patterns, (1, 1, 1, block))[..., : block * 2 * block]
    return repeated.reshape(sections, 2, heads, block, 2 * block)


def doc_masks(offsets, start, rows, block, seq_len):
    positions = start - block + jnp.arange(rows + 2 * block, dtype=jnp.int32)
    docs = jax.vmap(lambda o: doc_of(positions, o, seq_len))(offsets)
    groups, blocks = offsets.shape[0], rows // block
    tiles = docs.reshape(groups, blocks + 2, block)
    target = tiles[:, 1:-1]
    before = jnp.concatenate([tiles[:, :-2], target], axis=-1)
    after = jnp.concatenate([target, tiles[:, 2:]], axis=-1)
    window = jnp.stack([before, after])
    return (target[None, :, :, :, None] == window[:, :, :, None, :]).astype(jnp.bfloat16)


def paired(
    fwd_hidden,
    rev_hidden,
    bases,
    complement,
    offsets,
    base_embed,
    norm_gain,
    in_weight,
    filters,
    out_weight,
):
    rows, width = fwd_hidden.shape
    groups, ctx_count, parts = (lax.axis_size(a) for a in ("grp", "ctx", "ch"))
    mine, here, place = (lax.axis_index(a) for a in ("grp", "ctx", "ch"))
    sections, heads, block = filters.shape
    seq_len = rows * ctx_count
    half = width // groups

    columns = lax.dynamic_slice_in_dim(in_weight, mine * half, half, axis=2)
    early = lax.all_gather(columns[:sections], "ctx", axis=0)
    late = lax.all_gather(columns[sections:], "ctx", axis=0)
    near = lax.all_gather(
        lax.dynamic_slice_in_dim(out_weight, mine * half, half, axis=0), "ctx", axis=0
    )
    far = flip(near, "grp", 1)

    letters = base_embed.shape[0]
    alphabet = jnp.arange(letters, dtype=jnp.int32)
    onehot = (bases[:, None] == alphabet[None, :]).astype(jnp.bfloat16)
    swap_table = (complement[:, None] == alphabet[None, :]).astype(jnp.bfloat16)
    swapped = jnp.dot(swap_table, base_embed, preferred_element_type=jnp.float32)
    inputs = []
    for hidden, table in ((fwd_hidden, base_embed), (rev_hidden, swapped.astype(jnp.bfloat16))):
        embed = jnp.dot(onehot, table, preferred_element_type=jnp.float32)
        inputs.append((hidden.astype(jnp.float32) + embed).astype(jnp.bfloat16))
    other_x = [flip(v, "ch", 2) for v in inputs]
    other_y = [flip(v, "grp", 1) for v in inputs]
    other_xy = [flip(other_x[0], "grp", 1), flip(other_y[1], "ch", 2)]
    pieces = []
    for s in range(2):
        own = [inputs[s], flip(inputs[s], "ch", 1), other_x[s], flip(other_x[s], "ch", 1)]
        far_side = [other_y[s], flip(other_y[s], "ch", 1), other_xy[s], flip(other_xy[s], "ch", 1)]
        pieces.append([own, far_side])
    where = place.astype(jnp.int32).reshape(1)
    normed = norm_all(where, norm_gain, pieces, rows, width, parts)

    both_offsets = jnp.stack([offsets, flip(offsets, "grp", 1)])
    mask = doc_masks(both_offsets, here * rows, rows, block, seq_len)
    own_heads = heads // groups
    taps = lax.dynamic_slice_in_dim(filters, mine * own_heads, own_heads, axis=1)
    tables = conv_tables(taps.astype(jnp.bfloat16))

    state, *rims = first(normed, early, block)
    gate = gates(normed, early)
    for section in range(sections):
        rims = (shifted(rims[0], "ctx", 1), shifted(rims[1], "ctx", -1))
        if section + 1 < sections:
            state, *rims = conv_section(state, rims, tables, mask, section, gate[section])
        else:
            (conv,) = conv_section(state, rims, tables, mask, section)
    mixed_far = mix(normed, late, conv, 1)
    mixed_near = mix(normed, late, conv, 0)
    from_y = flip(mixed_far, "grp", 1)
    from_xy = across(mixed_far, 2)
    from_x = flip(mixed_near, "ch", 2)
    near_pieces = [mixed_near, flip(mixed_near, "ch", 1), from_x, flip(from_x, "ch", 1)]
    far_pieces = [from_y, flip(from_y, "ch", 1), from_xy, flip(from_xy, "ch", 1)]
    return project_out(where, near, far, near_pieces + far_pieces)


def solution(mesh):
    in_specs = (
        P(("grp", "ctx"), "ch"),
        P(("grp", "ctx"), "ch"),
        P(("grp", "ctx")),
        P(),
        P("grp"),
        P(None, "ch"),
        P(),
        P(None, "ctx", "ch"),
        P(None, "ch", None),
        P("ctx", "ch"),
    )
    out_specs = P(("grp", "ctx"), "ch")
    sizes = [mesh.shape[a] for a in ("grp", "ctx", "ch")]
    body = paired if sizes[0] == 2 and sizes[1] == sizes[2] == 4 else local
    return jax.shard_map(body, mesh=mesh, in_specs=in_specs, out_specs=out_specs, check_vma=False)
```

```python
import functools

import jax
import jax.numpy as jnp
from jax import lax
from jax.experimental import pallas as pl
from jax.experimental.pallas import tpu as pltpu
from jax.sharding import PartitionSpec as P

VMEM_LIMIT = 40 * 1024 * 1024
WIDE = 56 * 1024 * 1024
SMALL = pl.CostEstimate(flops=1, bytes_accessed=1, transcendentals=0)


def partner(block, axis, apart):
    count = lax.axis_size(axis)
    route = []
    for low in range(count):
        high = low | 1 << apart
        if high != low and high < count:
            route += [(low, high), (high, low)]
    return lax.ppermute(block, axis, route)


def shifted(value, axis, by):
    count = lax.axis_size(axis)
    pairs = [(i, i + by) for i in range(count) if 0 <= i + by < count]
    return lax.ppermute(value, axis, pairs)


def doc_of(positions, offsets, seq_len):
    count = jnp.sum((offsets[None, :] <= positions[:, None]).astype(jnp.int32), axis=1) - 1
    inside = (positions >= 0) & (positions < seq_len)
    return jnp.where(inside, count, -1)


def toeplitz(taps):
    heads, block = taps.shape
    pattern = jnp.concatenate(
        [jnp.zeros((heads, 1), taps.dtype), taps[:, ::-1], jnp.zeros((heads, block), taps.dtype)],
        axis=1,
    )
    repeated = jnp.tile(pattern, (1, block))
    return repeated[:, : block * 2 * block].reshape(heads, block, 2 * block)


def rms_norm(values, gain):
    floats = values.astype(jnp.float32)
    scale = lax.rsqrt(jnp.mean(floats * floats, axis=-1, keepdims=True) + 1e-05)
    return (floats * scale * gain).astype(jnp.bfloat16)


def blockwise_conv(conv_in, rim, taps, ext_docs):
    rows, width = conv_in.shape
    heads, block = taps.shape
    head_dim = width // heads
    blocks = rows // block
    extended = jnp.concatenate([rim, conv_in], axis=0)
    target_docs = ext_docs[block:].reshape(blocks, block)
    window = jnp.concatenate(
        [
            extended[:rows].reshape(blocks, block, width),
            extended[block:].reshape(blocks, block, width),
        ],
        axis=1,
    )
    window = window.reshape(blocks, 2 * block, heads, head_dim)
    window_docs = jnp.concatenate(
        [ext_docs[:rows].reshape(blocks, block), ext_docs[block:].reshape(blocks, block)], axis=1
    )
    mask = (target_docs[:, :, None] == window_docs[:, None, :]).astype(jnp.bfloat16)
    kernel = toeplitz(taps)[None] * mask[:, None]
    result = jnp.einsum("nhts,nshd->nthd", kernel, window, preferred_element_type=jnp.float32)
    return result.reshape(rows, width)


def local(
    fwd_hidden,
    rev_hidden,
    bases,
    complement,
    offsets,
    base_embed,
    norm_gain,
    in_weight,
    filters,
    out_weight,
):
    rows, width_local = fwd_hidden.shape
    ctx_count = lax.axis_size("ctx")
    here = lax.axis_index("ctx")
    seq_len = rows * ctx_count
    letters = base_embed.shape[0]
    alphabet = jnp.arange(letters, dtype=jnp.int32)
    onehot = (bases[:, None] == alphabet[None, :]).astype(jnp.bfloat16)
    swap_table = (complement[:, None] == alphabet[None, :]).astype(jnp.bfloat16)
    onehot_rev = jnp.dot(onehot, swap_table, preferred_element_type=jnp.float32).astype(
        jnp.bfloat16
    )
    embed_fwd = jnp.dot(onehot, base_embed, preferred_element_type=jnp.float32)
    embed_rev = jnp.dot(onehot_rev, base_embed, preferred_element_type=jnp.float32)
    fwd_input = (fwd_hidden.astype(jnp.float32) + embed_fwd).astype(jnp.bfloat16)
    rev_input = (rev_hidden.astype(jnp.float32) + embed_rev).astype(jnp.bfloat16)
    levels = ctx_count.bit_length() - 1
    for level in range(levels):
        rev_input = partner(rev_input, "ctx", level)
    rev_input = rev_input[::-1]
    full_fwd, full_rev = (
        lax.all_gather(fwd_input, "ch", axis=1, tiled=True),
        lax.all_gather(rev_input, "ch", axis=1, tiled=True),
    )
    normed_fwd = rms_norm(full_fwd, norm_gain)
    normed_rev = rms_norm(full_rev, norm_gain)
    piece = lax.all_gather(in_weight, "ctx", axis=1, tiled=True)
    add_fwd = jnp.einsum("rd,bdc->brc", normed_fwd, piece, preferred_element_type=jnp.float32)
    add_rev = jnp.einsum("rd,bdc->brc", normed_rev, piece, preferred_element_type=jnp.float32)
    taps_all = filters.astype(jnp.bfloat16)
    block = filters.shape[-1]
    before = here * rows - block + jnp.arange(rows + block, dtype=jnp.int32)
    docs_fwd = doc_of(before, offsets, seq_len)
    docs_rev = doc_of(seq_len - 1 - before, offsets, seq_len)
    state_fwd = add_fwd[0]
    state_rev = add_rev[0]
    for section in range(filters.shape[0]):
        in_fwd = state_fwd.astype(jnp.bfloat16)
        in_rev = state_rev.astype(jnp.bfloat16)
        rim_fwd, rim_rev = shifted((in_fwd[-block:], in_rev[-block:]), "ctx", 1)
        conv_rev = blockwise_conv(in_rev, rim_rev, taps_all[section], docs_rev)
        conv_fwd = blockwise_conv(in_fwd, rim_fwd, taps_all[section], docs_fwd)
        state_fwd = add_fwd[section + 1] * conv_fwd
        state_rev = add_rev[section + 1] * conv_rev
    mixed_fwd = state_fwd.astype(jnp.bfloat16)
    mixed_rev = state_rev.astype(jnp.bfloat16)
    for level in range(levels):
        mixed_rev = partner(mixed_rev, "ctx", level)
    mixed_rev = mixed_rev[::-1]
    mixed_sum = (mixed_fwd.astype(jnp.float32) + mixed_rev.astype(jnp.float32)).astype(jnp.bfloat16)
    whole_sum = lax.all_gather(mixed_sum, "ch", axis=1, tiled=True)
    total = jnp.dot(
        whole_sum,
        lax.all_gather(out_weight, "ctx", axis=0, tiled=True),
        preferred_element_type=jnp.float32,
    )
    return total.astype(jnp.bfloat16)


def flip(block, axis, bit):
    count = lax.axis_size(axis)
    return lax.ppermute(block, axis, [(i, i ^ bit) for i in range(count)])


def across(block, bit):
    groups, count = lax.axis_size("grp"), lax.axis_size("ch")
    pairs = [
        (g * count + k, (g ^ 1) * count + (k ^ bit)) for g in range(groups) for k in range(count)
    ]
    return lax.ppermute(block, ("grp", "ch"), pairs)


def params(*semantics, limit=None):
    return pltpu.CompilerParams(
        dimension_semantics=semantics, vmem_limit_bytes=limit or VMEM_LIMIT
    )


def gathered(block):
    two = flip(block, "ctx", 2)
    return [block, flip(block, "ctx", 1), two, flip(two, "ctx", 1)]


def after(value, *others):
    return lax.optimization_barrier((value,) + others)[0]


def norm_kernel(layout, place, gain, *refs):
    out = refs[-1]
    for s, strand in enumerate(layout):
        for g, group in enumerate(strand):
            blocks = [refs[n][...] if at is None else refs[n][at] for n, at in group]
            width = blocks[0].shape[-1]
            model = width * len(blocks)
            floats = [p.astype(jnp.float32) for p in blocks]
            total = sum(f * f for f in floats)
            scale = lax.rsqrt(jnp.sum(total, axis=-1, keepdims=True) / model + 1e-05)
            for j, f in enumerate(floats):
                lanes = pl.ds(pl.multiple_of((place[0] ^ j) * width, width), width)
                out[s, g, :, lanes] = (f * scale * gain[:, lanes]).astype(jnp.bfloat16)


def norm_all(place, gain, layout, arrays):
    strands, groups, parts = len(layout), len(layout[0]), len(layout[0][0])
    rows, width = arrays[0].shape[-2:]
    tile = 128

    def spec(array):
        if array.ndim == 2:
            return pl.BlockSpec((tile, width), lambda i, p: (i, 0))
        return pl.BlockSpec((strands, tile, width), lambda i, p: (0, i, 0))

    shape = (strands, groups, rows, width * parts)
    return pl.pallas_call(
        functools.partial(norm_kernel, layout),
        grid_spec=pltpu.PrefetchScalarGridSpec(
            num_scalar_prefetch=1,
            grid=(rows // tile,),
            in_specs=[pl.BlockSpec((1, width * parts), lambda i, p: (0, 0))]
            + [spec(v) for v in arrays],
            out_specs=pl.BlockSpec(
                (strands, groups, tile, width * parts), lambda i, p: (0, 0, i, 0)
            ),
        ),
        out_shape=jax.ShapeDtypeStruct(shape, jnp.bfloat16),
        compiler_params=params("arbitrary"),
        cost_estimate=SMALL,
        name="norm",
    )(place, gain.reshape(1, -1), *arrays)


def project(normed, weight, b):
    count, _, depth, _ = weight.shape
    parts = [
        jnp.dot(
            normed[:, z * depth : (z + 1) * depth],
            weight[z, b],
            preferred_element_type=jnp.float32,
        )
        for z in range(count)
    ]
    return sum(parts[1:], parts[0])


def keep_rims(value, s, g, rim_fwd, rim_rev):
    rows, block = value.shape[0], rim_fwd.shape[1]

    @pl.when(s == 0)
    def _():
        rim_fwd[g] = value[rows - block :]

    @pl.when(s == 1)
    def _():
        rim_rev[g] = value[:block]


def first_kernel(normed, weight, state, rim_fwd, rim_rev):
    s, g = pl.program_id(0), pl.program_id(1)
    value = project(normed[0, 0], weight, 0).astype(jnp.bfloat16)
    state[0, 0] = value
    keep_rims(value, s, g, rim_fwd, rim_rev)


def first(normed, weight, block):
    strands, groups, rows, model = normed.shape
    count, few, depth, width = weight.shape
    rim = jax.ShapeDtypeStruct((groups, block, width), jnp.bfloat16)
    rim_spec = pl.BlockSpec((groups, block, width), lambda s, g: (0, 0, 0))
    return pl.pallas_call(
        first_kernel,
        grid=(strands, groups),
        in_specs=[
            pl.BlockSpec((1, 1, rows, model), lambda s, g: (s, g, 0, 0)),
            pl.BlockSpec((count, 1, depth, width), lambda s, g: (0, 0, 0, 0)),
        ],
        out_specs=[
            pl.BlockSpec((1, 1, rows, width), lambda s, g: (s, g, 0, 0)),
            rim_spec,
            rim_spec,
        ],
        out_shape=[
            jax.ShapeDtypeStruct((strands, groups, rows, width), jnp.bfloat16),
            rim,
            rim,
        ],
        compiler_params=params("arbitrary", "arbitrary", limit=WIDE),
        cost_estimate=SMALL,
        name="first",
    )(normed, weight)


def gate_kernel(normed, weight, out):
    out[0, 0] = project(normed[0, 0], weight, 0)


def gate_of(normed, weight, b):
    strands, groups, rows, model = normed.shape
    count, _, depth, width = weight.shape
    return pl.pallas_call(
        gate_kernel,
        grid=(strands, groups),
        in_specs=[
            pl.BlockSpec((1, 1, rows, model), lambda s, g: (s, g, 0, 0)),
            pl.BlockSpec((count, 1, depth, width), lambda s, g: (0, b, 0, 0)),
        ],
        out_specs=pl.BlockSpec((1, 1, rows, width), lambda s, g: (s, g, 0, 0)),
        out_shape=jax.ShapeDtypeStruct((strands, groups, rows, width), jnp.float32),
        compiler_params=params("arbitrary", "arbitrary"),
        cost_estimate=SMALL,
        name="gate",
    )(normed, weight)


def toeplitz_of(pattern, block):
    width = pattern.shape[-1]
    spread = jnp.broadcast_to(pattern, (block, width))
    return pltpu.roll(spread, 0, 1, stride=1, stride_axis=0).astype(jnp.bfloat16)


def conv_kernel(last, state, rim_fwd, rim_rev, patterns, mask, *refs):
    s, g = pl.program_id(0), pl.program_id(1)
    extended, table = refs[-2:]
    rows, width = state.shape[2:]
    block = rim_fwd.shape[1]
    heads = table.shape[0]
    head = width // heads

    @pl.when(s == 0)
    def _():
        extended[:block] = rim_fwd[g]
        extended[block:] = state[0, 0]

    @pl.when(s == 1)
    def _():
        extended[:rows] = state[0, 0]
        extended[rows:] = rim_rev[g]

    @pl.when(g == 0)
    def _():
        for h in range(heads):
            table[h] = toeplitz_of(patterns[0, 0, h], block)

    for n in range(rows // block):
        span = slice(n * block, (n + 1) * block)
        for h in range(heads):
            lanes = slice(h * head, (h + 1) * head)
            conv = jnp.dot(
                table[h] * mask[0, 0, n],
                extended[n * block : (n + 2) * block, lanes],
                preferred_element_type=jnp.float32,
            )
            if last:
                refs[0][0, 0, span, lanes] = conv
            else:
                refs[1][0, 0, span, lanes] = (refs[0][0, 0, span, lanes] * conv).astype(
                    jnp.bfloat16
                )
    if not last:
        keep_rims(refs[1][0, 0], s, g, refs[2], refs[3])


def conv_section(state, rims, patterns, mask, section, gate=None):
    strands, groups, rows, width = state.shape
    heads = patterns.shape[2]
    block = rims[0].shape[1]
    rim = jax.ShapeDtypeStruct((groups, block, width), jnp.bfloat16)
    rim_spec = pl.BlockSpec((groups, block, width), lambda s, g: (0, 0, 0))
    row_spec = pl.BlockSpec((1, 1, rows, width), lambda s, g: (s, g, 0, 0))
    last = gate is None
    in_specs = [
        row_spec,
        rim_spec,
        rim_spec,
        pl.BlockSpec((1, 1, heads, 1, 2 * block), lambda s, g: (section, s, 0, 0, 0)),
        pl.BlockSpec((1, 1, rows // block, block, 2 * block), lambda s, g: (s, g, 0, 0, 0)),
    ]
    args = [state, rims[0], rims[1], patterns, mask]
    if last:
        out_specs = [row_spec]
        out_shape = [jax.ShapeDtypeStruct(state.shape, jnp.float32)]
    else:
        in_specs.append(row_spec)
        args.append(gate)
        out_specs = [row_spec, rim_spec, rim_spec]
        out_shape = [jax.ShapeDtypeStruct(state.shape, jnp.bfloat16), rim, rim]
    return pl.pallas_call(
        functools.partial(conv_kernel, last),
        grid=(strands, groups),
        in_specs=in_specs,
        out_specs=out_specs,
        out_shape=out_shape,
        scratch_shapes=[
            pltpu.VMEM((rows + block, width), jnp.bfloat16),
            pltpu.VMEM((heads, block, 2 * block), jnp.bfloat16),
        ],
        compiler_params=params("arbitrary", "arbitrary"),
        cost_estimate=SMALL,
        name="conv",
    )(*args)


def mix_kernel(normed, weight, conv, near, far):
    total = None
    for s in range(normed.shape[0]):
        gate = project(normed[s, 0], weight, 0)
        state = (gate * conv[s, 0]).astype(jnp.bfloat16).astype(jnp.float32)
        total = state if total is None else total + state
    total = total.astype(jnp.bfloat16)

    @pl.when(pl.program_id(0) == 0)
    def _():
        far[...] = total

    @pl.when(pl.program_id(0) == 1)
    def _():
        near[...] = total


def mix(normed, weight, conv):
    strands, groups, rows, model = normed.shape
    count, _, depth, width = weight.shape
    shape = jax.ShapeDtypeStruct((rows, width), jnp.bfloat16)
    return pl.pallas_call(
        mix_kernel,
        grid=(groups,),
        in_specs=[
            pl.BlockSpec((strands, 1, rows, model), lambda g: (0, 1 - g, 0, 0)),
            pl.BlockSpec((count, 1, depth, width), lambda g: (0, 0, 0, 0)),
            pl.BlockSpec((strands, 1, rows, width), lambda g: (0, 1 - g, 0, 0)),
        ],
        out_specs=[pl.BlockSpec((rows, width), lambda g: (0, 0))] * 2,
        out_shape=[shape, shape],
        compiler_params=params("arbitrary", limit=WIDE),
        cost_estimate=SMALL,
        name="mix",
    )(normed, weight, conv)


def out_kernel(spots, weight, *refs):
    pieces, out = refs[:-1], refs[-1]
    parts = len(pieces) // 2
    deep = pieces[0].shape[1]
    total = None
    for n, piece in enumerate(pieces):
        group = spots[1] if n < parts else 1 - spots[1]
        rows = pl.ds(pl.multiple_of(group * deep, deep), deep)
        term = jnp.dot(
            piece[...],
            weight[spots[0] ^ (n % parts), rows, :],
            preferred_element_type=jnp.float32,
        )
        total = term if total is None else total + term
    out[...] = total.astype(jnp.bfloat16)


def project_out(spots, weight, pieces):
    rows, deep = pieces[0].shape
    width = weight.shape[-1]
    tile = rows // 2
    return pl.pallas_call(
        out_kernel,
        grid_spec=pltpu.PrefetchScalarGridSpec(
            num_scalar_prefetch=1,
            grid=(rows // tile,),
            in_specs=[pl.BlockSpec(weight.shape, lambda i, p: (0, 0, 0))]
            + [pl.BlockSpec((tile, deep), lambda i, p: (i, 0)) for _ in pieces],
            out_specs=pl.BlockSpec((tile, width), lambda i, p: (i, 0)),
        ),
        out_shape=jax.ShapeDtypeStruct((rows, width), jnp.bfloat16),
        compiler_params=params("arbitrary"),
        cost_estimate=SMALL,
        name="out",
    )(spots, weight, *pieces)


def conv_patterns(taps):
    zero = jnp.zeros_like(taps)
    forward = jnp.concatenate([zero[..., :1], taps[..., ::-1], zero[..., 1:]], axis=-1)
    reverse = jnp.concatenate([taps, zero], axis=-1)
    return jnp.stack([forward, reverse], axis=1)[:, :, :, None, :]


def doc_masks(offsets, start, rows, block, seq_len):
    positions = start - block + jnp.arange(rows + 2 * block, dtype=jnp.int32)
    docs = jax.vmap(lambda o: doc_of(positions, o, seq_len))(offsets)
    groups, blocks = offsets.shape[0], rows // block
    tiles = docs.reshape(groups, blocks + 2, block)
    target = tiles[:, 1:-1]
    before = jnp.concatenate([tiles[:, :-2], target], axis=-1)
    after = jnp.concatenate([target, tiles[:, 2:]], axis=-1)
    window = jnp.stack([before, after])
    return (target[None, :, :, :, None] == window[:, :, :, None, :]).astype(jnp.bfloat16)


def paired(
    fwd_hidden,
    rev_hidden,
    bases,
    complement,
    offsets,
    base_embed,
    norm_gain,
    in_weight,
    filters,
    out_weight,
):
    rows, width = fwd_hidden.shape
    groups, ctx_count, parts = (lax.axis_size(a) for a in ("grp", "ctx", "ch"))
    mine, here, place = (lax.axis_index(a) for a in ("grp", "ctx", "ch"))
    sections, heads, block = filters.shape
    seq_len = rows * ctx_count
    half = width // groups

    columns = lax.dynamic_slice_in_dim(in_weight, mine * half, half, axis=2)
    early = lax.all_gather(columns[:sections], "ctx", axis=0)

    letters = base_embed.shape[0]
    alphabet = jnp.arange(letters, dtype=jnp.int32)
    onehot = (bases[:, None] == alphabet[None, :]).astype(jnp.bfloat16)
    swap_table = (complement[:, None] == alphabet[None, :]).astype(jnp.bfloat16)
    swapped = jnp.dot(swap_table, base_embed, preferred_element_type=jnp.float32)
    inputs = []
    for hidden, table in ((fwd_hidden, base_embed), (rev_hidden, swapped.astype(jnp.bfloat16))):
        embed = jnp.dot(onehot, table, preferred_element_type=jnp.float32)
        inputs.append((hidden.astype(jnp.float32) + embed).astype(jnp.bfloat16))
    own = jnp.stack(inputs)
    x = flip(own, "ch", 2)
    y = flip(own, "grp", 1)
    core = flip(own, "ch", 1)
    x, y, core = lax.optimization_barrier((x, y, core))
    xy = [flip(x[0], "grp", 1), flip(y[1], "ch", 2)]
    arrays = [own, core, x, flip(x, "ch", 1), y, flip(y, "ch", 1)]
    arrays += [xy[0], flip(xy[0], "ch", 1), xy[1], flip(xy[1], "ch", 1)]
    layout = [
        [
            [(n, s) for n in range(1, 5)],
            [(5, s), (6, s), (7 + 2 * s, None), (8 + 2 * s, None)],
        ]
        for s in range(2)
    ]
    layout = [[[(n - 1, at) for n, at in group] for group in strand] for strand in layout]
    spots = jnp.stack([place, mine]).astype(jnp.int32)
    normed = norm_all(spots, norm_gain, layout, arrays)
    late = lax.all_gather(after(columns[sections:], x), "ctx", axis=0)
    both_offsets = jnp.stack([offsets, flip(offsets, "grp", 1)])
    mask = doc_masks(both_offsets, here * rows, rows, block, seq_len)
    own_heads = heads // groups
    taps = lax.dynamic_slice_in_dim(filters, mine * own_heads, own_heads, axis=1)
    patterns = conv_patterns(taps.astype(jnp.bfloat16).astype(jnp.float32))

    def shift_rims(rims):
        return shifted(rims[0], "ctx", 1), shifted(rims[1], "ctx", -1)

    early, normed, mask, patterns = lax.optimization_barrier((early, normed, mask, patterns))
    whole_out = lax.all_gather(after(out_weight, early), "ctx", axis=0)
    state, *rims = first(normed, early, block)
    rims = shift_rims(rims)
    gate = gate_of(normed, early, 1)
    state, *rims = conv_section(state, rims, patterns, mask, 0, gate)
    state, normed = lax.optimization_barrier((state, normed))
    rims = shift_rims(rims)
    gate = gate_of(normed, early, 2)
    state, *rims = conv_section(state, rims, patterns, mask, 1, gate)
    rims = shift_rims(rims)
    (conv,) = conv_section(state, rims, patterns, mask, 2)
    mixed_near, mixed_far = mix(normed, late, conv)
    from_y = flip(mixed_far, "grp", 1)
    from_xy = across(mixed_far, 2)
    from_x = flip(mixed_near, "ch", 2)
    near_pieces = [mixed_near, flip(mixed_near, "ch", 1), from_x, flip(from_x, "ch", 1)]
    far_pieces = [from_y, flip(from_y, "ch", 1), from_xy, flip(from_xy, "ch", 1)]
    return project_out(spots, whole_out, near_pieces + far_pieces)


def solution(mesh):
    in_specs = (
        P(("grp", "ctx"), "ch"),
        P(("grp", "ctx"), "ch"),
        P(("grp", "ctx")),
        P(),
        P("grp"),
        P(None, "ch"),
        P(),
        P(None, "ctx", "ch"),
        P(None, "ch", None),
        P("ctx", "ch"),
    )
    out_specs = P(("grp", "ctx"), "ch")
    sizes = [mesh.shape[a] for a in ("grp", "ctx", "ch")]
    body = paired if sizes[0] == 2 and sizes[1] == sizes[2] == 4 else local
    return jax.shard_map(body, mesh=mesh, in_specs=in_specs, out_specs=out_specs, check_vma=False)
```

```python
import functools

import jax
import jax.numpy as jnp
from jax import lax
from jax.experimental import pallas as pl
from jax.experimental.pallas import tpu as pltpu
from jax.sharding import PartitionSpec as P

VMEM_LIMIT = 40 * 1024 * 1024
WIDE = 56 * 1024 * 1024
SMALL = pl.CostEstimate(flops=1, bytes_accessed=1, transcendentals=0)


def partner(block, axis, apart):
    count = lax.axis_size(axis)
    route = []
    for low in range(count):
        high = low | 1 << apart
        if high != low and high < count:
            route += [(low, high), (high, low)]
    return lax.ppermute(block, axis, route)


def shifted(value, axis, by):
    count = lax.axis_size(axis)
    pairs = [(i, i + by) for i in range(count) if 0 <= i + by < count]
    return lax.ppermute(value, axis, pairs)


def doc_of(positions, offsets, seq_len):
    count = jnp.sum((offsets[None, :] <= positions[:, None]).astype(jnp.int32), axis=1) - 1
    inside = (positions >= 0) & (positions < seq_len)
    return jnp.where(inside, count, -1)


def toeplitz(taps):
    heads, block = taps.shape
    pattern = jnp.concatenate(
        [jnp.zeros((heads, 1), taps.dtype), taps[:, ::-1], jnp.zeros((heads, block), taps.dtype)],
        axis=1,
    )
    repeated = jnp.tile(pattern, (1, block))
    return repeated[:, : block * 2 * block].reshape(heads, block, 2 * block)


def rms_norm(values, gain):
    floats = values.astype(jnp.float32)
    scale = lax.rsqrt(jnp.mean(floats * floats, axis=-1, keepdims=True) + 1e-05)
    return (floats * scale * gain).astype(jnp.bfloat16)


def blockwise_conv(conv_in, rim, taps, ext_docs):
    rows, width = conv_in.shape
    heads, block = taps.shape
    head_dim = width // heads
    blocks = rows // block
    extended = jnp.concatenate([rim, conv_in], axis=0)
    target_docs = ext_docs[block:].reshape(blocks, block)
    window = jnp.concatenate(
        [
            extended[:rows].reshape(blocks, block, width),
            extended[block:].reshape(blocks, block, width),
        ],
        axis=1,
    )
    window = window.reshape(blocks, 2 * block, heads, head_dim)
    window_docs = jnp.concatenate(
        [ext_docs[:rows].reshape(blocks, block), ext_docs[block:].reshape(blocks, block)], axis=1
    )
    mask = (target_docs[:, :, None] == window_docs[:, None, :]).astype(jnp.bfloat16)
    kernel = toeplitz(taps)[None] * mask[:, None]
    result = jnp.einsum("nhts,nshd->nthd", kernel, window, preferred_element_type=jnp.float32)
    return result.reshape(rows, width)


def local(
    fwd_hidden,
    rev_hidden,
    bases,
    complement,
    offsets,
    base_embed,
    norm_gain,
    in_weight,
    filters,
    out_weight,
):
    rows, width_local = fwd_hidden.shape
    ctx_count = lax.axis_size("ctx")
    here = lax.axis_index("ctx")
    seq_len = rows * ctx_count
    letters = base_embed.shape[0]
    alphabet = jnp.arange(letters, dtype=jnp.int32)
    onehot = (bases[:, None] == alphabet[None, :]).astype(jnp.bfloat16)
    swap_table = (complement[:, None] == alphabet[None, :]).astype(jnp.bfloat16)
    onehot_rev = jnp.dot(onehot, swap_table, preferred_element_type=jnp.float32).astype(
        jnp.bfloat16
    )
    embed_fwd = jnp.dot(onehot, base_embed, preferred_element_type=jnp.float32)
    embed_rev = jnp.dot(onehot_rev, base_embed, preferred_element_type=jnp.float32)
    fwd_input = (fwd_hidden.astype(jnp.float32) + embed_fwd).astype(jnp.bfloat16)
    rev_input = (rev_hidden.astype(jnp.float32) + embed_rev).astype(jnp.bfloat16)
    levels = ctx_count.bit_length() - 1
    for level in range(levels):
        rev_input = partner(rev_input, "ctx", level)
    rev_input = rev_input[::-1]
    full_fwd, full_rev = (
        lax.all_gather(fwd_input, "ch", axis=1, tiled=True),
        lax.all_gather(rev_input, "ch", axis=1, tiled=True),
    )
    normed_fwd = rms_norm(full_fwd, norm_gain)
    normed_rev = rms_norm(full_rev, norm_gain)
    piece = lax.all_gather(in_weight, "ctx", axis=1, tiled=True)
    add_fwd = jnp.einsum("rd,bdc->brc", normed_fwd, piece, preferred_element_type=jnp.float32)
    add_rev = jnp.einsum("rd,bdc->brc", normed_rev, piece, preferred_element_type=jnp.float32)
    taps_all = filters.astype(jnp.bfloat16)
    block = filters.shape[-1]
    before = here * rows - block + jnp.arange(rows + block, dtype=jnp.int32)
    docs_fwd = doc_of(before, offsets, seq_len)
    docs_rev = doc_of(seq_len - 1 - before, offsets, seq_len)
    state_fwd = add_fwd[0]
    state_rev = add_rev[0]
    for section in range(filters.shape[0]):
        in_fwd = state_fwd.astype(jnp.bfloat16)
        in_rev = state_rev.astype(jnp.bfloat16)
        rim_fwd, rim_rev = shifted((in_fwd[-block:], in_rev[-block:]), "ctx", 1)
        conv_rev = blockwise_conv(in_rev, rim_rev, taps_all[section], docs_rev)
        conv_fwd = blockwise_conv(in_fwd, rim_fwd, taps_all[section], docs_fwd)
        state_fwd = add_fwd[section + 1] * conv_fwd
        state_rev = add_rev[section + 1] * conv_rev
    mixed_fwd = state_fwd.astype(jnp.bfloat16)
    mixed_rev = state_rev.astype(jnp.bfloat16)
    for level in range(levels):
        mixed_rev = partner(mixed_rev, "ctx", level)
    mixed_rev = mixed_rev[::-1]
    mixed_sum = (mixed_fwd.astype(jnp.float32) + mixed_rev.astype(jnp.float32)).astype(jnp.bfloat16)
    whole_sum = lax.all_gather(mixed_sum, "ch", axis=1, tiled=True)
    total = jnp.dot(
        whole_sum,
        lax.all_gather(out_weight, "ctx", axis=0, tiled=True),
        preferred_element_type=jnp.float32,
    )
    return total.astype(jnp.bfloat16)


def flip(block, axis, bit):
    count = lax.axis_size(axis)
    return lax.ppermute(block, axis, [(i, i ^ bit) for i in range(count)])


def across(block, bit):
    groups, count = lax.axis_size("grp"), lax.axis_size("ch")
    pairs = [
        (g * count + k, (g ^ 1) * count + (k ^ bit)) for g in range(groups) for k in range(count)
    ]
    return lax.ppermute(block, ("grp", "ch"), pairs)


def params(*semantics, limit=None):
    return pltpu.CompilerParams(
        dimension_semantics=semantics, vmem_limit_bytes=limit or VMEM_LIMIT
    )


def gathered(block):
    two = flip(block, "ctx", 2)
    return [block, flip(block, "ctx", 1), two, flip(two, "ctx", 1)]


def after(value, *others):
    return lax.optimization_barrier((value,) + others)[0]


def norm_kernel(layout, place, gain, *refs):
    out = refs[-1]
    for s, strand in enumerate(layout):
        for g, group in enumerate(strand):
            blocks = [refs[n][...] if at is None else refs[n][at] for n, at in group]
            width = blocks[0].shape[-1]
            model = width * len(blocks)
            floats = [p.astype(jnp.float32) for p in blocks]
            total = sum(f * f for f in floats)
            scale = lax.rsqrt(jnp.sum(total, axis=-1, keepdims=True) / model + 1e-05)
            for j, f in enumerate(floats):
                lanes = pl.ds(pl.multiple_of((place[0] ^ j) * width, width), width)
                out[s, g, :, lanes] = (f * scale * gain[:, lanes]).astype(jnp.bfloat16)


def norm_all(place, gain, layout, arrays):
    strands, groups, parts = len(layout), len(layout[0]), len(layout[0][0])
    rows, width = arrays[0].shape[-2:]
    tile = 128

    def spec(array):
        if array.ndim == 2:
            return pl.BlockSpec((tile, width), lambda i, p: (i, 0))
        return pl.BlockSpec((strands, tile, width), lambda i, p: (0, i, 0))

    shape = (strands, groups, rows, width * parts)
    return pl.pallas_call(
        functools.partial(norm_kernel, layout),
        grid_spec=pltpu.PrefetchScalarGridSpec(
            num_scalar_prefetch=1,
            grid=(rows // tile,),
            in_specs=[pl.BlockSpec((1, width * parts), lambda i, p: (0, 0))]
            + [spec(v) for v in arrays],
            out_specs=pl.BlockSpec(
                (strands, groups, tile, width * parts), lambda i, p: (0, 0, i, 0)
            ),
        ),
        out_shape=jax.ShapeDtypeStruct(shape, jnp.bfloat16),
        compiler_params=params("arbitrary"),
        cost_estimate=SMALL,
        name="norm",
    )(place, gain.reshape(1, -1), *arrays)


CUTS = 4


def fetch(normed, weight, count, order, held, kept, x_sems, w_sems):
    depth = weight.shape[2]
    for b in range(count):
        for z in range(weight.shape[0]):
            span = pl.ds(z * depth, depth)
            pltpu.make_async_copy(
                weight.at[z, b], kept.at[b, span], w_sems.at[b, z]
            ).start()
    groups, rows = normed.shape[1:3]
    part = rows // CUTS
    for s, g in order:
        at = s * groups + g
        for c in range(CUTS):
            span = pl.ds(c * part, part)
            pltpu.make_async_copy(
                normed.at[s, g, span], held.at[at, span], x_sems.at[at, c]
            ).start()


def wait_weight(weight, count, kept, w_sems):
    depth = weight.shape[2]
    for b in range(count):
        for z in range(weight.shape[0]):
            span = pl.ds(z * depth, depth)
            pltpu.make_async_copy(weight.at[z, 0], kept.at[b, span], w_sems.at[b, z]).wait()


def wait_rows(normed, at, held, x_sems):
    part = normed.shape[2] // CUTS
    for c in range(CUTS):
        span = pl.ds(c * part, part)
        pltpu.make_async_copy(normed.at[0, 0, span], held.at[at, span], x_sems.at[at, c]).wait()


def product(value, weight):
    return jnp.dot(value[...], weight[...], preferred_element_type=jnp.float32)


def fetch_scratch(normed, weight, count):
    strands, groups, rows, model = normed.shape
    blocks, _, depth, width = weight.shape
    return [
        pltpu.VMEM((strands * groups, rows, model), jnp.bfloat16),
        pltpu.VMEM((count, blocks * depth, width), jnp.bfloat16),
        pltpu.SemaphoreType.DMA((strands * groups, CUTS)),
        pltpu.SemaphoreType.DMA((count, blocks)),
    ]


def toeplitz_of(pattern, block):
    width = pattern.shape[-1]
    spread = jnp.broadcast_to(pattern, (block, width))
    return pltpu.roll(spread, 0, 1, stride=1, stride_axis=0).astype(jnp.bfloat16)


def tables_kernel(patterns, tables):
    block = tables.shape[-2]
    for k in range(tables.shape[0]):
        for h in range(tables.shape[2]):
            tables[k, 0, h] = toeplitz_of(patterns[k, 0, h], block)


def tables_of(patterns):
    sections, strands, heads, _, width = patterns.shape
    block = width // 2
    return pl.pallas_call(
        tables_kernel,
        grid=(strands,),
        in_specs=[pl.BlockSpec((sections, 1, heads, 1, width), lambda s: (0, s, 0, 0, 0))],
        out_specs=pl.BlockSpec((sections, 1, heads, block, width), lambda s: (0, s, 0, 0, 0)),
        out_shape=jax.ShapeDtypeStruct((sections, strands, heads, block, width), jnp.bfloat16),
        compiler_params=params("arbitrary"),
        cost_estimate=SMALL,
        name="tables",
    )(patterns)


def gated_block(k, s, n, blocks, window, table, mask, gate, gate_at=None):
    block = table.shape[-2]
    place = jnp.where(s == 0, n, blocks - 1 - n)
    at = pl.multiple_of(place * block, block)
    heads = table.shape[2]
    head = gate.shape[-1] // heads
    gate_at = at if gate_at is None else gate_at
    out = []
    for h in range(heads):
        lanes = slice(h * head, (h + 1) * head)
        conv = jnp.dot(
            table[k, 0, h] * mask[0, 0, place],
            window[pl.ds(at, 2 * block), lanes],
            preferred_element_type=jnp.float32,
        )
        out.append((gate[pl.ds(gate_at, block), lanes] * conv).astype(jnp.bfloat16))
    return at, jnp.concatenate(out, axis=-1)


def shifted_at(at, s, block):
    return pl.multiple_of(at + jnp.where(s == 0, block, 0), block)


def early_kernel(normed, weight, table, mask, *refs):
    s, g = pl.program_id(0), pl.program_id(1)
    states, gates_out, rim_fwd, rim_rev = refs[:4]
    held, kept, x_sems, w_sems, *extended = refs[4:8] + refs[8:10]
    gates = refs[10:]
    groups, rows = normed.shape[1:3]
    block = table.shape[-2]
    blocks = rows // block

    @pl.when((s == 0) & (g == 0))
    def _():
        order = [(i, j) for i in range(normed.shape[0]) for j in range(groups)]
        fetch(normed, weight, 3, order, held, kept, x_sems, w_sems)
        wait_weight(weight, 3, kept, w_sems)

    def row_of(n):
        return pl.multiple_of(jnp.where(s == 0, n, blocks - 1 - n) * block, block)

    def keep_rim(k, value):
        @pl.when(s == 0)
        def _():
            rim_fwd[k, g] = value

        @pl.when(s == 1)
        def _():
            rim_rev[k, g] = value

    at = s * groups + g
    wait_rows(normed, at, held, x_sems)
    extended[0][pl.ds(shifted_at(0, s, block), rows)] = product(
        held.at[at], kept.at[0]
    ).astype(jnp.bfloat16)
    states[0, 0, 0] = extended[0][pl.ds(shifted_at(row_of(0), s, block), block)]
    keep_rim(0, extended[0][pl.ds(shifted_at(row_of(blocks - 1), s, block), block)])
    for k in range(2):
        gates[k][...] = product(held.at[at], kept.at[k + 1])
    gates_out[0, 0, 0] = gates[0][pl.ds(row_of(0), block)]
    for n in range(2):
        gates_out[0, 0, 1 + n] = gates[1][pl.ds(row_of(n), block)]
    for n in range(1, blocks):
        row, value = gated_block(0, s, n, blocks, extended[0], table, mask, gates[0])
        extended[1][pl.ds(shifted_at(row, s, block), block)] = value
        if n == 1:
            states[0, 0, 1] = value
    keep_rim(1, value)
    for n in range(2, blocks):
        row, value = gated_block(1, s, n, blocks, extended[1], table, mask, gates[1])
        states[0, 0, n] = value
    keep_rim(2, value)


def early_sections(normed, weight, tables, mask):
    strands, groups, rows, _ = normed.shape
    width = weight.shape[-1]
    sections, _, heads, block, _ = tables.shape
    blocks = rows // block
    rim = jax.ShapeDtypeStruct((sections, groups, block, width), jnp.bfloat16)
    rim_spec = pl.BlockSpec(rim.shape, lambda s, g: (0, 0, 0, 0))
    return pl.pallas_call(
        early_kernel,
        grid=(strands, groups),
        in_specs=[pl.BlockSpec(memory_space=pltpu.HBM)] * 2
        + [
            pl.BlockSpec((sections, 1, heads, block, 2 * block), lambda s, g: (0, s, 0, 0, 0)),
            pl.BlockSpec((1, 1, blocks, block, 2 * block), lambda s, g: (s, g, 0, 0, 0)),
        ],
        out_specs=[
            pl.BlockSpec((1, 1, blocks, block, width), lambda s, g: (s, g, 0, 0, 0)),
            pl.BlockSpec((1, 1, 3, block, width), lambda s, g: (s, g, 0, 0, 0)),
            rim_spec,
            rim_spec,
        ],
        out_shape=[
            jax.ShapeDtypeStruct((strands, groups, blocks, block, width), jnp.bfloat16),
            jax.ShapeDtypeStruct((strands, groups, 3, block, width), jnp.float32),
            rim,
            rim,
        ],
        scratch_shapes=fetch_scratch(normed, weight, 3)
        + [pltpu.VMEM((rows + block, width), jnp.bfloat16)] * 2
        + [pltpu.VMEM((rows, width), jnp.float32)] * 2,
        compiler_params=params("arbitrary", "arbitrary", limit=WIDE),
        cost_estimate=SMALL,
        name="early_sections",
    )(normed, weight, tables, mask)


def late_kernel(g, normed, weight, states, gates, table, mask, *refs):
    rims, out = refs[:2], refs[2]
    held, kept, x_sems, w_sems, last_gate, *extended = refs[3:]
    s = pl.program_id(0)
    groups, rows = normed.shape[1:3]
    block = table.shape[-2]
    blocks = rows // block

    @pl.when(s == 0)
    def _():
        order = [(i, g) for i in range(normed.shape[0])]
        fetch(normed, weight, 1, order, held, kept, x_sems, w_sems)

    def put(k, n, value):
        at = jnp.where(s == 0, n, blocks - 1 - n) * block
        extended[k][pl.ds(shifted_at(at, s, block), block)] = value

    for k in range(3):

        @pl.when(s == 0)
        def _():
            extended[k][:block] = rims[0][k, 0]

        @pl.when(s == 1)
        def _():
            extended[k][rows:] = rims[1][k, 0]

    put(0, 0, states[0, 0, 0])
    put(1, 1, states[0, 0, 1])
    for n in range(2, blocks):
        put(2, n, states[0, 0, n])
    for k in range(2):
        for n in range(k + 1):
            gate = gates.at[0, 0, k + n]
            _, value = gated_block(k, s, n, blocks, extended[k], table, mask, gate, 0)
            put(k + 1, n, value)

    @pl.when(s == 0)
    def _():
        wait_weight(weight, 1, kept, w_sems)

    at = s * groups + g
    wait_rows(normed, at, held, x_sems)
    last_gate[...] = product(held.at[at], kept.at[0])
    for n in range(blocks):
        row, value = gated_block(2, s, n, blocks, extended[2], table, mask, last_gate)
        span = pl.ds(row, block)
        before = jnp.where(s == 0, 0.0, out[span].astype(jnp.float32))
        out[span] = (before + value.astype(jnp.float32)).astype(jnp.bfloat16)


def late_sections(normed, weight, states, gates, tables, mask, rims, g):
    strands, groups, rows, _ = normed.shape
    blocks, block, width = states.shape[2:]
    sections, _, heads = tables.shape[:3]
    return pl.pallas_call(
        functools.partial(late_kernel, g),
        grid=(strands,),
        in_specs=[pl.BlockSpec(memory_space=pltpu.HBM)] * 2
        + [
            pl.BlockSpec((1, 1, blocks, block, width), lambda s: (s, g, 0, 0, 0)),
            pl.BlockSpec((1, 1, 3, block, width), lambda s: (s, g, 0, 0, 0)),
            pl.BlockSpec((sections, 1, heads, block, 2 * block), lambda s: (0, s, 0, 0, 0)),
            pl.BlockSpec((1, 1, blocks, block, 2 * block), lambda s: (s, g, 0, 0, 0)),
        ]
        + [pl.BlockSpec((sections, 1, block, width), lambda s: (0, g, 0, 0)) for _ in rims],
        out_specs=pl.BlockSpec((rows, width), lambda s: (0, 0)),
        out_shape=jax.ShapeDtypeStruct((rows, width), jnp.bfloat16),
        scratch_shapes=fetch_scratch(normed, weight, 1)
        + [pltpu.VMEM((rows, width), jnp.float32)]
        + [pltpu.VMEM((rows + block, width), jnp.bfloat16)] * 3,
        compiler_params=params("arbitrary", limit=WIDE),
        cost_estimate=SMALL,
        name="late_sections",
    )(normed, weight, states, gates, tables, mask, *rims)


def out_kernel(parts, spots, *refs):
    weights, pieces = refs[: 2 * parts], refs[2 * parts : -2]
    out, held = refs[-2:]

    @pl.when(pl.program_id(0) == 0)
    def _():
        for half in range(2):
            for i in range(parts):
                held[half, spots[1] ^ i] = weights[half * parts + i][...]

    total = None
    for half in range(2):
        for j in range(parts):
            piece = pieces[half * parts + j]
            term = jnp.dot(
                piece[...], held[half, spots[0] ^ j], preferred_element_type=jnp.float32
            )
            total = term if total is None else total + term
    out[...] = total.astype(jnp.bfloat16)


def project_out(spots, near, far, pieces):
    parts = len(near)
    rows, depth = pieces[0].shape
    width = near[0].shape[-1]
    tile = rows // 2
    return pl.pallas_call(
        functools.partial(out_kernel, parts),
        grid_spec=pltpu.PrefetchScalarGridSpec(
            num_scalar_prefetch=1,
            grid=(rows // tile,),
            in_specs=[pl.BlockSpec(w.shape, lambda i, p: (0, 0)) for w in near + far]
            + [pl.BlockSpec((tile, depth), lambda i, p: (i, 0)) for _ in pieces],
            out_specs=pl.BlockSpec((tile, width), lambda i, p: (i, 0)),
            scratch_shapes=[pltpu.VMEM((2, parts, depth, width), jnp.bfloat16)],
        ),
        out_shape=jax.ShapeDtypeStruct((rows, width), jnp.bfloat16),
        compiler_params=params("arbitrary"),
        cost_estimate=SMALL,
        name="out",
    )(spots, *near, *far, *pieces)


def conv_patterns(taps):
    zero = jnp.zeros_like(taps)
    forward = jnp.concatenate([zero[..., :1], taps[..., ::-1], zero[..., 1:]], axis=-1)
    reverse = jnp.concatenate([taps, zero], axis=-1)
    return jnp.stack([forward, reverse], axis=1)[:, :, :, None, :]


def doc_masks(offsets, start, rows, block, seq_len):
    positions = start - block + jnp.arange(rows + 2 * block, dtype=jnp.int32)
    docs = jax.vmap(lambda o: doc_of(positions, o, seq_len))(offsets)
    groups, blocks = offsets.shape[0], rows // block
    tiles = docs.reshape(groups, blocks + 2, block)
    target = tiles[:, 1:-1]
    before = jnp.concatenate([tiles[:, :-2], target], axis=-1)
    after = jnp.concatenate([target, tiles[:, 2:]], axis=-1)
    window = jnp.stack([before, after])
    return (target[None, :, :, :, None] == window[:, :, :, None, :]).astype(jnp.bfloat16)


def paired(
    fwd_hidden,
    rev_hidden,
    bases,
    complement,
    offsets,
    base_embed,
    norm_gain,
    in_weight,
    filters,
    out_weight,
):
    rows, width = fwd_hidden.shape
    groups, ctx_count, parts = (lax.axis_size(a) for a in ("grp", "ctx", "ch"))
    mine, here, place = (lax.axis_index(a) for a in ("grp", "ctx", "ch"))
    sections, heads, block = filters.shape
    seq_len = rows * ctx_count
    half = width // groups

    columns = lax.dynamic_slice_in_dim(in_weight, mine * half, half, axis=2)
    early = lax.all_gather(columns[:sections], "ctx", axis=0)

    letters = base_embed.shape[0]
    alphabet = jnp.arange(letters, dtype=jnp.int32)
    onehot = (bases[:, None] == alphabet[None, :]).astype(jnp.bfloat16)
    swap_table = (complement[:, None] == alphabet[None, :]).astype(jnp.bfloat16)
    swapped = jnp.dot(swap_table, base_embed, preferred_element_type=jnp.float32)
    inputs = []
    for hidden, table in ((fwd_hidden, base_embed), (rev_hidden, swapped.astype(jnp.bfloat16))):
        embed = jnp.dot(onehot, table, preferred_element_type=jnp.float32)
        inputs.append((hidden.astype(jnp.float32) + embed).astype(jnp.bfloat16))
    own = jnp.stack(inputs)
    x = flip(own, "ch", 2)
    y = flip(own, "grp", 1)
    core = flip(own, "ch", 1)
    x, y, core = lax.optimization_barrier((x, y, core))
    xy = [flip(x[0], "grp", 1), flip(y[1], "ch", 2)]
    arrays = [own, core, x, flip(x, "ch", 1), y, flip(y, "ch", 1)]
    arrays += [xy[0], flip(xy[0], "ch", 1), xy[1], flip(xy[1], "ch", 1)]
    layout = [
        [
            [(n, s) for n in range(1, 5)],
            [(5, s), (6, s), (7 + 2 * s, None), (8 + 2 * s, None)],
        ]
        for s in range(2)
    ]
    layout = [[[(n - 1, at) for n, at in group] for group in strand] for strand in layout]
    spots = jnp.stack([place, here]).astype(jnp.int32)
    normed = norm_all(spots, norm_gain, layout, arrays)
    late = lax.all_gather(after(columns[sections:], x), "ctx", axis=0)

    both_offsets = jnp.stack([offsets, flip(offsets, "grp", 1)])
    mask = doc_masks(both_offsets, here * rows, rows, block, seq_len)
    own_heads = heads // groups
    taps = lax.dynamic_slice_in_dim(filters, mine * own_heads, own_heads, axis=1)
    patterns = conv_patterns(taps.astype(jnp.bfloat16).astype(jnp.float32))

    tables = tables_of(patterns)
    out_near = lax.dynamic_slice_in_dim(out_weight, mine * half, half, axis=0)
    out_far = lax.dynamic_slice_in_dim(out_weight, (1 - mine) * half, half, axis=0)
    early, normed, mask, tables, out_near = lax.optimization_barrier(
        (early, normed, mask, tables, out_near)
    )
    one, two = flip(out_near, "ctx", 1), flip(out_near, "ctx", 2)
    states, gates, rim_fwd, rim_rev = early_sections(normed, early, tables, mask)
    rims = shifted(rim_fwd, "ctx", 1), shifted(rim_rev, "ctx", -1)
    one, two, states = lax.optimization_barrier((one, two, states))
    near = [out_near, one, two, flip(two, "ctx", 1)]
    far = [out_far] + [flip(w, "grp", 1) for w in near[1:]]
    work = normed, late, states, gates, tables, mask, rims
    mixed_far = late_sections(*work, 1)
    mixed_near = late_sections(*work, 0)
    from_y = flip(mixed_far, "grp", 1)
    from_xy = across(mixed_far, 2)
    from_x = flip(mixed_near, "ch", 2)
    near_pieces = [mixed_near, flip(mixed_near, "ch", 1), from_x, flip(from_x, "ch", 1)]
    far_pieces = [from_y, flip(from_y, "ch", 1), from_xy, flip(from_xy, "ch", 1)]
    return project_out(spots, near, far, near_pieces + far_pieces)


def solution(mesh):
    in_specs = (
        P(("grp", "ctx"), "ch"),
        P(("grp", "ctx"), "ch"),
        P(("grp", "ctx")),
        P(),
        P("grp"),
        P(None, "ch"),
        P(),
        P(None, "ctx", "ch"),
        P(None, "ch", None),
        P("ctx", "ch"),
    )
    out_specs = P(("grp", "ctx"), "ch")
    sizes = [mesh.shape[a] for a in ("grp", "ctx", "ch")]
    body = paired if sizes[0] == 2 and sizes[1] == sizes[2] == 4 else local
    return jax.shard_map(body, mesh=mesh, in_specs=in_specs, out_specs=out_specs, check_vma=False)
```

```python
import functools

import jax
import jax.numpy as jnp
from jax import lax
from jax.experimental import pallas as pl
from jax.experimental.pallas import tpu as pltpu
from jax.sharding import PartitionSpec as P

VMEM_LIMIT = 40 * 1024 * 1024
WIDE = 56 * 1024 * 1024
SMALL = pl.CostEstimate(flops=1, bytes_accessed=1, transcendentals=0)


def partner(block, axis, apart):
    count = lax.axis_size(axis)
    route = []
    for low in range(count):
        high = low | 1 << apart
        if high != low and high < count:
            route += [(low, high), (high, low)]
    return lax.ppermute(block, axis, route)


def shifted(value, axis, by):
    count = lax.axis_size(axis)
    pairs = [(i, i + by) for i in range(count) if 0 <= i + by < count]
    return lax.ppermute(value, axis, pairs)


def doc_of(positions, offsets, seq_len):
    count = jnp.sum((offsets[None, :] <= positions[:, None]).astype(jnp.int32), axis=1) - 1
    inside = (positions >= 0) & (positions < seq_len)
    return jnp.where(inside, count, -1)


def toeplitz(taps):
    heads, block = taps.shape
    pattern = jnp.concatenate(
        [jnp.zeros((heads, 1), taps.dtype), taps[:, ::-1], jnp.zeros((heads, block), taps.dtype)],
        axis=1,
    )
    repeated = jnp.tile(pattern, (1, block))
    return repeated[:, : block * 2 * block].reshape(heads, block, 2 * block)


def rms_norm(values, gain):
    floats = values.astype(jnp.float32)
    scale = lax.rsqrt(jnp.mean(floats * floats, axis=-1, keepdims=True) + 1e-05)
    return (floats * scale * gain).astype(jnp.bfloat16)


def blockwise_conv(conv_in, rim, taps, ext_docs):
    rows, width = conv_in.shape
    heads, block = taps.shape
    head_dim = width // heads
    blocks = rows // block
    extended = jnp.concatenate([rim, conv_in], axis=0)
    target_docs = ext_docs[block:].reshape(blocks, block)
    window = jnp.concatenate(
        [
            extended[:rows].reshape(blocks, block, width),
            extended[block:].reshape(blocks, block, width),
        ],
        axis=1,
    )
    window = window.reshape(blocks, 2 * block, heads, head_dim)
    window_docs = jnp.concatenate(
        [ext_docs[:rows].reshape(blocks, block), ext_docs[block:].reshape(blocks, block)], axis=1
    )
    mask = (target_docs[:, :, None] == window_docs[:, None, :]).astype(jnp.bfloat16)
    kernel = toeplitz(taps)[None] * mask[:, None]
    result = jnp.einsum("nhts,nshd->nthd", kernel, window, preferred_element_type=jnp.float32)
    return result.reshape(rows, width)


def local(
    fwd_hidden,
    rev_hidden,
    bases,
    complement,
    offsets,
    base_embed,
    norm_gain,
    in_weight,
    filters,
    out_weight,
):
    rows, width_local = fwd_hidden.shape
    ctx_count = lax.axis_size("ctx")
    here = lax.axis_index("ctx")
    seq_len = rows * ctx_count
    letters = base_embed.shape[0]
    alphabet = jnp.arange(letters, dtype=jnp.int32)
    onehot = (bases[:, None] == alphabet[None, :]).astype(jnp.bfloat16)
    swap_table = (complement[:, None] == alphabet[None, :]).astype(jnp.bfloat16)
    onehot_rev = jnp.dot(onehot, swap_table, preferred_element_type=jnp.float32).astype(
        jnp.bfloat16
    )
    embed_fwd = jnp.dot(onehot, base_embed, preferred_element_type=jnp.float32)
    embed_rev = jnp.dot(onehot_rev, base_embed, preferred_element_type=jnp.float32)
    fwd_input = (fwd_hidden.astype(jnp.float32) + embed_fwd).astype(jnp.bfloat16)
    rev_input = (rev_hidden.astype(jnp.float32) + embed_rev).astype(jnp.bfloat16)
    levels = ctx_count.bit_length() - 1
    for level in range(levels):
        rev_input = partner(rev_input, "ctx", level)
    rev_input = rev_input[::-1]
    full_fwd, full_rev = (
        lax.all_gather(fwd_input, "ch", axis=1, tiled=True),
        lax.all_gather(rev_input, "ch", axis=1, tiled=True),
    )
    normed_fwd = rms_norm(full_fwd, norm_gain)
    normed_rev = rms_norm(full_rev, norm_gain)
    piece = lax.all_gather(in_weight, "ctx", axis=1, tiled=True)
    add_fwd = jnp.einsum("rd,bdc->brc", normed_fwd, piece, preferred_element_type=jnp.float32)
    add_rev = jnp.einsum("rd,bdc->brc", normed_rev, piece, preferred_element_type=jnp.float32)
    taps_all = filters.astype(jnp.bfloat16)
    block = filters.shape[-1]
    before = here * rows - block + jnp.arange(rows + block, dtype=jnp.int32)
    docs_fwd = doc_of(before, offsets, seq_len)
    docs_rev = doc_of(seq_len - 1 - before, offsets, seq_len)
    state_fwd = add_fwd[0]
    state_rev = add_rev[0]
    for section in range(filters.shape[0]):
        in_fwd = state_fwd.astype(jnp.bfloat16)
        in_rev = state_rev.astype(jnp.bfloat16)
        rim_fwd, rim_rev = shifted((in_fwd[-block:], in_rev[-block:]), "ctx", 1)
        conv_rev = blockwise_conv(in_rev, rim_rev, taps_all[section], docs_rev)
        conv_fwd = blockwise_conv(in_fwd, rim_fwd, taps_all[section], docs_fwd)
        state_fwd = add_fwd[section + 1] * conv_fwd
        state_rev = add_rev[section + 1] * conv_rev
    mixed_fwd = state_fwd.astype(jnp.bfloat16)
    mixed_rev = state_rev.astype(jnp.bfloat16)
    for level in range(levels):
        mixed_rev = partner(mixed_rev, "ctx", level)
    mixed_rev = mixed_rev[::-1]
    mixed_sum = (mixed_fwd.astype(jnp.float32) + mixed_rev.astype(jnp.float32)).astype(jnp.bfloat16)
    whole_sum = lax.all_gather(mixed_sum, "ch", axis=1, tiled=True)
    total = jnp.dot(
        whole_sum,
        lax.all_gather(out_weight, "ctx", axis=0, tiled=True),
        preferred_element_type=jnp.float32,
    )
    return total.astype(jnp.bfloat16)


def flip(block, axis, bit):
    count = lax.axis_size(axis)
    return lax.ppermute(block, axis, [(i, i ^ bit) for i in range(count)])


def across(block, bit):
    groups, count = lax.axis_size("grp"), lax.axis_size("ch")
    pairs = [
        (g * count + k, (g ^ 1) * count + (k ^ bit)) for g in range(groups) for k in range(count)
    ]
    return lax.ppermute(block, ("grp", "ch"), pairs)


def params(*semantics, limit=None):
    return pltpu.CompilerParams(
        dimension_semantics=semantics, vmem_limit_bytes=limit or VMEM_LIMIT
    )


def gathered(block):
    two = flip(block, "ctx", 2)
    return [block, flip(block, "ctx", 1), two, flip(two, "ctx", 1)]


def after(value, *others):
    return lax.optimization_barrier((value,) + others)[0]


def norm_kernel(layout, place, gain, *refs):
    out = refs[-1]
    for s, strand in enumerate(layout):
        for g, group in enumerate(strand):
            blocks = [refs[n][...] if at is None else refs[n][at] for n, at in group]
            width = blocks[0].shape[-1]
            model = width * len(blocks)
            floats = [p.astype(jnp.float32) for p in blocks]
            total = sum(f * f for f in floats)
            scale = lax.rsqrt(jnp.sum(total, axis=-1, keepdims=True) / model + 1e-05)
            for j, f in enumerate(floats):
                lanes = pl.ds(pl.multiple_of((place[0] ^ j) * width, width), width)
                out[s, g, :, lanes] = (f * scale * gain[:, lanes]).astype(jnp.bfloat16)


def norm_all(place, gain, layout, arrays):
    strands, groups, parts = len(layout), len(layout[0]), len(layout[0][0])
    rows, width = arrays[0].shape[-2:]
    tile = 128

    def spec(array):
        if array.ndim == 2:
            return pl.BlockSpec((tile, width), lambda i, p: (i, 0))
        return pl.BlockSpec((strands, tile, width), lambda i, p: (0, i, 0))

    shape = (strands, groups, rows, width * parts)
    return pl.pallas_call(
        functools.partial(norm_kernel, layout),
        grid_spec=pltpu.PrefetchScalarGridSpec(
            num_scalar_prefetch=1,
            grid=(rows // tile,),
            in_specs=[pl.BlockSpec((1, width * parts), lambda i, p: (0, 0))]
            + [spec(v) for v in arrays],
            out_specs=pl.BlockSpec(
                (strands, groups, tile, width * parts), lambda i, p: (0, 0, i, 0)
            ),
        ),
        out_shape=jax.ShapeDtypeStruct(shape, jnp.bfloat16),
        compiler_params=params("arbitrary"),
        cost_estimate=SMALL,
        name="norm",
    )(place, gain.reshape(1, -1), *arrays)


CUTS = 4


def fetch(normed, weight, count, order, held, kept, x_sems, w_sems):
    depth = weight.shape[2]
    for b in range(count):
        for z in range(weight.shape[0]):
            span = pl.ds(z * depth, depth)
            pltpu.make_async_copy(
                weight.at[z, b], kept.at[b, span], w_sems.at[b, z]
            ).start()
    groups, rows = normed.shape[1:3]
    part = rows // CUTS
    for s, g in order:
        at = s * groups + g
        for c in range(CUTS):
            span = pl.ds(c * part, part)
            pltpu.make_async_copy(
                normed.at[s, g, span], held.at[at, span], x_sems.at[at, c]
            ).start()


def wait_weight(weight, count, kept, w_sems):
    depth = weight.shape[2]
    for b in range(count):
        for z in range(weight.shape[0]):
            span = pl.ds(z * depth, depth)
            pltpu.make_async_copy(weight.at[z, 0], kept.at[b, span], w_sems.at[b, z]).wait()


def wait_rows(normed, at, held, x_sems):
    part = normed.shape[2] // CUTS
    for c in range(CUTS):
        span = pl.ds(c * part, part)
        pltpu.make_async_copy(normed.at[0, 0, span], held.at[at, span], x_sems.at[at, c]).wait()


def product(value, weight):
    return jnp.dot(value[...], weight[...], preferred_element_type=jnp.float32)


def fetch_scratch(normed, weight, count):
    strands, groups, rows, model = normed.shape
    blocks, _, depth, width = weight.shape
    return [
        pltpu.VMEM((strands * groups, rows, model), jnp.bfloat16),
        pltpu.VMEM((count, blocks * depth, width), jnp.bfloat16),
        pltpu.SemaphoreType.DMA((strands * groups, CUTS)),
        pltpu.SemaphoreType.DMA((count, blocks)),
    ]


def toeplitz_of(pattern, block):
    width = pattern.shape[-1]
    spread = jnp.broadcast_to(pattern, (block, width))
    return pltpu.roll(spread, 0, 1, stride=1, stride_axis=0).astype(jnp.bfloat16)


def tables_kernel(patterns, tables):
    block = tables.shape[-2]
    for k in range(tables.shape[0]):
        for h in range(tables.shape[2]):
            tables[k, 0, h] = toeplitz_of(patterns[k, 0, h], block)


def tables_of(patterns):
    sections, strands, heads, _, width = patterns.shape
    block = width // 2
    return pl.pallas_call(
        tables_kernel,
        grid=(strands,),
        in_specs=[pl.BlockSpec((sections, 1, heads, 1, width), lambda s: (0, s, 0, 0, 0))],
        out_specs=pl.BlockSpec((sections, 1, heads, block, width), lambda s: (0, s, 0, 0, 0)),
        out_shape=jax.ShapeDtypeStruct((sections, strands, heads, block, width), jnp.bfloat16),
        compiler_params=params("arbitrary"),
        cost_estimate=SMALL,
        name="tables",
    )(patterns)


def gated_block(k, s, n, blocks, window, table, mask, gate, gate_at=None):
    block = table.shape[-2]
    place = jnp.where(s == 0, n, blocks - 1 - n)
    at = pl.multiple_of(place * block, block)
    heads = table.shape[2]
    head = gate.shape[-1] // heads
    gate_at = at if gate_at is None else gate_at
    out = []
    for h in range(heads):
        lanes = slice(h * head, (h + 1) * head)
        conv = jnp.dot(
            table[k, 0, h] * mask[0, 0, place],
            window[pl.ds(at, 2 * block), lanes],
            preferred_element_type=jnp.float32,
        )
        out.append((gate[pl.ds(gate_at, block), lanes] * conv).astype(jnp.bfloat16))
    return at, jnp.concatenate(out, axis=-1)


def shifted_at(at, s, block):
    return pl.multiple_of(at + jnp.where(s == 0, block, 0), block)


def early_kernel(normed, weight, table, mask, *refs):
    s, g = pl.program_id(0), pl.program_id(1)
    states, gates_out, rim_fwd, rim_rev = refs[:4]
    held, kept, x_sems, w_sems, *extended = refs[4:8] + refs[8:10]
    gates = refs[10:]
    groups, rows = normed.shape[1:3]
    block = table.shape[-2]
    blocks = rows // block

    @pl.when((s == 0) & (g == 0))
    def _():
        order = [(i, j) for i in range(normed.shape[0]) for j in range(groups)]
        fetch(normed, weight, 3, order, held, kept, x_sems, w_sems)
        wait_weight(weight, 3, kept, w_sems)

    def row_of(n):
        return pl.multiple_of(jnp.where(s == 0, n, blocks - 1 - n) * block, block)

    def keep_rim(k, value):
        @pl.when(s == 0)
        def _():
            rim_fwd[k, g] = value

        @pl.when(s == 1)
        def _():
            rim_rev[k, g] = value

    at = s * groups + g
    wait_rows(normed, at, held, x_sems)
    extended[0][pl.ds(shifted_at(0, s, block), rows)] = product(
        held.at[at], kept.at[0]
    ).astype(jnp.bfloat16)
    states[0, 0, 0] = extended[0][pl.ds(shifted_at(row_of(0), s, block), block)]
    keep_rim(0, extended[0][pl.ds(shifted_at(row_of(blocks - 1), s, block), block)])
    for k in range(2):
        gates[k][...] = product(held.at[at], kept.at[k + 1])
    gates_out[0, 0, 0] = gates[0][pl.ds(row_of(0), block)]
    for n in range(2):
        gates_out[0, 0, 1 + n] = gates[1][pl.ds(row_of(n), block)]
    for n in range(1, blocks):
        row, value = gated_block(0, s, n, blocks, extended[0], table, mask, gates[0])
        extended[1][pl.ds(shifted_at(row, s, block), block)] = value
        if n == 1:
            states[0, 0, 1] = value
    keep_rim(1, value)
    for n in range(2, blocks):
        row, value = gated_block(1, s, n, blocks, extended[1], table, mask, gates[1])
        states[0, 0, n] = value
    keep_rim(2, value)


def early_sections(normed, weight, tables, mask):
    strands, groups, rows, _ = normed.shape
    width = weight.shape[-1]
    sections, _, heads, block, _ = tables.shape
    blocks = rows // block
    rim = jax.ShapeDtypeStruct((sections, groups, block, width), jnp.bfloat16)
    rim_spec = pl.BlockSpec(rim.shape, lambda s, g: (0, 0, 0, 0))
    return pl.pallas_call(
        early_kernel,
        grid=(strands, groups),
        in_specs=[pl.BlockSpec(memory_space=pltpu.HBM)] * 2
        + [
            pl.BlockSpec((sections, 1, heads, block, 2 * block), lambda s, g: (0, s, 0, 0, 0)),
            pl.BlockSpec((1, 1, blocks, block, 2 * block), lambda s, g: (s, g, 0, 0, 0)),
        ],
        out_specs=[
            pl.BlockSpec((1, 1, blocks, block, width), lambda s, g: (s, g, 0, 0, 0)),
            pl.BlockSpec((1, 1, 3, block, width), lambda s, g: (s, g, 0, 0, 0)),
            rim_spec,
            rim_spec,
        ],
        out_shape=[
            jax.ShapeDtypeStruct((strands, groups, blocks, block, width), jnp.bfloat16),
            jax.ShapeDtypeStruct((strands, groups, 3, block, width), jnp.float32),
            rim,
            rim,
        ],
        scratch_shapes=fetch_scratch(normed, weight, 3)
        + [pltpu.VMEM((rows + block, width), jnp.bfloat16)] * 2
        + [pltpu.VMEM((rows, width), jnp.float32)] * 2,
        compiler_params=params("arbitrary", "arbitrary", limit=WIDE),
        cost_estimate=SMALL,
        name="early_sections",
    )(normed, weight, tables, mask)


def late_kernel(g, normed, weight, states, gates, table, mask, *refs):
    rims, out = refs[:2], refs[2]
    held, kept, x_sems, w_sems, last_gate, *extended = refs[3:]
    s = pl.program_id(0)
    groups, rows = normed.shape[1:3]
    block = table.shape[-2]
    blocks = rows // block

    @pl.when(s == 0)
    def _():
        order = [(i, g) for i in range(normed.shape[0])]
        fetch(normed, weight, 1, order, held, kept, x_sems, w_sems)

    def put(k, n, value):
        at = jnp.where(s == 0, n, blocks - 1 - n) * block
        extended[k][pl.ds(shifted_at(at, s, block), block)] = value

    for k in range(3):

        @pl.when(s == 0)
        def _():
            extended[k][:block] = rims[0][k, 0]

        @pl.when(s == 1)
        def _():
            extended[k][rows:] = rims[1][k, 0]

    put(0, 0, states[0, 0, 0])
    put(1, 1, states[0, 0, 1])
    for n in range(2, blocks):
        put(2, n, states[0, 0, n])
    for k in range(2):
        for n in range(k + 1):
            gate = gates.at[0, 0, k + n]
            _, value = gated_block(k, s, n, blocks, extended[k], table, mask, gate, 0)
            put(k + 1, n, value)

    @pl.when(s == 0)
    def _():
        wait_weight(weight, 1, kept, w_sems)

    at = s * groups + g
    wait_rows(normed, at, held, x_sems)
    last_gate[...] = product(held.at[at], kept.at[0])
    for n in range(blocks):
        row, value = gated_block(2, s, n, blocks, extended[2], table, mask, last_gate)
        span = pl.ds(row, block)
        before = jnp.where(s == 0, 0.0, out[span].astype(jnp.float32))
        out[span] = (before + value.astype(jnp.float32)).astype(jnp.bfloat16)


def late_sections(normed, weight, states, gates, tables, mask, rims, g):
    strands, groups, rows, _ = normed.shape
    blocks, block, width = states.shape[2:]
    sections, _, heads = tables.shape[:3]
    return pl.pallas_call(
        functools.partial(late_kernel, g),
        grid=(strands,),
        in_specs=[pl.BlockSpec(memory_space=pltpu.HBM)] * 2
        + [
            pl.BlockSpec((1, 1, blocks, block, width), lambda s: (s, g, 0, 0, 0)),
            pl.BlockSpec((1, 1, 3, block, width), lambda s: (s, g, 0, 0, 0)),
            pl.BlockSpec((sections, 1, heads, block, 2 * block), lambda s: (0, s, 0, 0, 0)),
            pl.BlockSpec((1, 1, blocks, block, 2 * block), lambda s: (s, g, 0, 0, 0)),
        ]
        + [pl.BlockSpec((sections, 1, block, width), lambda s: (0, g, 0, 0)) for _ in rims],
        out_specs=pl.BlockSpec((rows, width), lambda s: (0, 0)),
        out_shape=jax.ShapeDtypeStruct((rows, width), jnp.bfloat16),
        scratch_shapes=fetch_scratch(normed, weight, 1)
        + [pltpu.VMEM((rows, width), jnp.float32)]
        + [pltpu.VMEM((rows + block, width), jnp.bfloat16)] * 3,
        compiler_params=params("arbitrary", limit=WIDE),
        cost_estimate=SMALL,
        name="late_sections",
    )(normed, weight, states, gates, tables, mask, *rims)


def last_gate_kernel(g, normed, weight, out, held, kept, x_sems, w_sems):
    s = pl.program_id(0)

    @pl.when(s == 0)
    def _():
        order = [(i, g) for i in range(normed.shape[0])]
        fetch(normed, weight, 1, order, held, kept, x_sems, w_sems)
        wait_weight(weight, 1, kept, w_sems)

    at = s * normed.shape[1] + g
    wait_rows(normed, at, held, x_sems)
    out[0] = product(held.at[at], kept.at[0])


def last_gate_of(normed, weight, g):
    strands, _, rows, _ = normed.shape
    width = weight.shape[-1]
    return pl.pallas_call(
        functools.partial(last_gate_kernel, g),
        grid=(strands,),
        in_specs=[pl.BlockSpec(memory_space=pltpu.HBM)] * 2,
        out_specs=pl.BlockSpec((1, rows, width), lambda s: (s, 0, 0)),
        out_shape=jax.ShapeDtypeStruct((strands, rows, width), jnp.float32),
        scratch_shapes=fetch_scratch(normed, weight, 1),
        compiler_params=params("arbitrary", limit=WIDE),
        cost_estimate=SMALL,
        name="last_gate",
    )(normed, weight)


def gated_kernel(last_gate, states, gates, table, mask, *refs):
    rims, out = refs[:2], refs[2]
    extended = refs[3:]
    s = pl.program_id(0)
    block = table.shape[-2]
    rows = out.shape[0]
    blocks = rows // block

    def put(k, n, value):
        at = jnp.where(s == 0, n, blocks - 1 - n) * block
        extended[k][pl.ds(shifted_at(at, s, block), block)] = value

    for k in range(3):

        @pl.when(s == 0)
        def _():
            extended[k][:block] = rims[0][k, 0]

        @pl.when(s == 1)
        def _():
            extended[k][rows:] = rims[1][k, 0]

    put(0, 0, states[0, 0, 0])
    put(1, 1, states[0, 0, 1])
    for n in range(2, blocks):
        put(2, n, states[0, 0, n])
    for k in range(2):
        for n in range(k + 1):
            gate = gates.at[0, 0, k + n]
            _, value = gated_block(k, s, n, blocks, extended[k], table, mask, gate, 0)
            put(k + 1, n, value)

    for n in range(blocks):
        row, value = gated_block(2, s, n, blocks, extended[2], table, mask, last_gate.at[0])
        span = pl.ds(row, block)
        before = jnp.where(s == 0, 0.0, out[span].astype(jnp.float32))
        out[span] = (before + value.astype(jnp.float32)).astype(jnp.bfloat16)


def gated_sections(last_gate, states, gates, tables, mask, rims, g):
    strands, rows, _ = last_gate.shape
    blocks, block, width = states.shape[2:]
    sections, _, heads = tables.shape[:3]
    return pl.pallas_call(
        gated_kernel,
        grid=(strands,),
        in_specs=[pl.BlockSpec((1, rows, width), lambda s: (s, 0, 0))]
        + [
            pl.BlockSpec((1, 1, blocks, block, width), lambda s: (s, g, 0, 0, 0)),
            pl.BlockSpec((1, 1, 3, block, width), lambda s: (s, g, 0, 0, 0)),
            pl.BlockSpec((sections, 1, heads, block, 2 * block), lambda s: (0, s, 0, 0, 0)),
            pl.BlockSpec((1, 1, blocks, block, 2 * block), lambda s: (s, g, 0, 0, 0)),
        ]
        + [pl.BlockSpec((sections, 1, block, width), lambda s: (0, g, 0, 0)) for _ in rims],
        out_specs=pl.BlockSpec((rows, width), lambda s: (0, 0)),
        out_shape=jax.ShapeDtypeStruct((rows, width), jnp.bfloat16),
        scratch_shapes=[pltpu.VMEM((rows + block, width), jnp.bfloat16)] * 3,
        compiler_params=params("arbitrary", limit=WIDE),
        cost_estimate=SMALL,
        name="gated_sections",
    )(last_gate, states, gates, tables, mask, *rims)


def out_kernel(parts, spots, *refs):
    weights, pieces = refs[: 2 * parts], refs[2 * parts : -2]
    out, held = refs[-2:]

    @pl.when(pl.program_id(0) == 0)
    def _():
        for half in range(2):
            for i in range(parts):
                held[half, spots[1] ^ i] = weights[half * parts + i][...]

    total = None
    for half in range(2):
        for j in range(parts):
            piece = pieces[half * parts + j]
            term = jnp.dot(
                piece[...], held[half, spots[0] ^ j], preferred_element_type=jnp.float32
            )
            total = term if total is None else total + term
    out[...] = total.astype(jnp.bfloat16)


def project_out(spots, near, far, pieces):
    parts = len(near)
    rows, depth = pieces[0].shape
    width = near[0].shape[-1]
    tile = rows
    return pl.pallas_call(
        functools.partial(out_kernel, parts),
        grid_spec=pltpu.PrefetchScalarGridSpec(
            num_scalar_prefetch=1,
            grid=(rows // tile,),
            in_specs=[pl.BlockSpec(w.shape, lambda i, p: (0, 0)) for w in near + far]
            + [pl.BlockSpec((tile, depth), lambda i, p: (i, 0)) for _ in pieces],
            out_specs=pl.BlockSpec((tile, width), lambda i, p: (i, 0)),
            scratch_shapes=[pltpu.VMEM((2, parts, depth, width), jnp.bfloat16)],
        ),
        out_shape=jax.ShapeDtypeStruct((rows, width), jnp.bfloat16),
        compiler_params=params("arbitrary"),
        cost_estimate=SMALL,
        name="out",
    )(spots, *near, *far, *pieces)


def conv_patterns(taps):
    zero = jnp.zeros_like(taps)
    forward = jnp.concatenate([zero[..., :1], taps[..., ::-1], zero[..., 1:]], axis=-1)
    reverse = jnp.concatenate([taps, zero], axis=-1)
    return jnp.stack([forward, reverse], axis=1)[:, :, :, None, :]


def doc_masks(offsets, start, rows, block, seq_len):
    positions = start - block + jnp.arange(rows + 2 * block, dtype=jnp.int32)
    docs = jax.vmap(lambda o: doc_of(positions, o, seq_len))(offsets)
    groups, blocks = offsets.shape[0], rows // block
    tiles = docs.reshape(groups, blocks + 2, block)
    target = tiles[:, 1:-1]
    before = jnp.concatenate([tiles[:, :-2], target], axis=-1)
    after = jnp.concatenate([target, tiles[:, 2:]], axis=-1)
    window = jnp.stack([before, after])
    return (target[None, :, :, :, None] == window[:, :, :, None, :]).astype(jnp.bfloat16)


def paired(
    fwd_hidden,
    rev_hidden,
    bases,
    complement,
    offsets,
    base_embed,
    norm_gain,
    in_weight,
    filters,
    out_weight,
):
    rows, width = fwd_hidden.shape
    groups, ctx_count, parts = (lax.axis_size(a) for a in ("grp", "ctx", "ch"))
    mine, here, place = (lax.axis_index(a) for a in ("grp", "ctx", "ch"))
    sections, heads, block = filters.shape
    seq_len = rows * ctx_count
    half = width // groups

    columns = lax.dynamic_slice_in_dim(in_weight, mine * half, half, axis=2)
    early = lax.all_gather(columns[:sections], "ctx", axis=0)

    letters = base_embed.shape[0]
    alphabet = jnp.arange(letters, dtype=jnp.int32)
    onehot = (bases[:, None] == alphabet[None, :]).astype(jnp.bfloat16)
    swap_table = (complement[:, None] == alphabet[None, :]).astype(jnp.bfloat16)
    swapped = jnp.dot(swap_table, base_embed, preferred_element_type=jnp.float32)
    inputs = []
    for hidden, table in ((fwd_hidden, base_embed), (rev_hidden, swapped.astype(jnp.bfloat16))):
        embed = jnp.dot(onehot, table, preferred_element_type=jnp.float32)
        inputs.append((hidden.astype(jnp.float32) + embed).astype(jnp.bfloat16))
    own = jnp.stack(inputs)
    x = flip(own, "ch", 2)
    y = flip(own, "grp", 1)
    core = flip(own, "ch", 1)
    x, y, core = lax.optimization_barrier((x, y, core))
    xy = [flip(x[0], "grp", 1), flip(y[1], "ch", 2)]
    arrays = [own, core, x, flip(x, "ch", 1), y, flip(y, "ch", 1)]
    arrays += [xy[0], flip(xy[0], "ch", 1), xy[1], flip(xy[1], "ch", 1)]
    layout = [
        [
            [(n, s) for n in range(1, 5)],
            [(5, s), (6, s), (7 + 2 * s, None), (8 + 2 * s, None)],
        ]
        for s in range(2)
    ]
    layout = [[[(n - 1, at) for n, at in group] for group in strand] for strand in layout]
    spots = jnp.stack([place, here]).astype(jnp.int32)
    normed = norm_all(spots, norm_gain, layout, arrays)
    late = lax.all_gather(after(columns[sections:], x), "ctx", axis=0)

    both_offsets = jnp.stack([offsets, flip(offsets, "grp", 1)])
    mask = doc_masks(both_offsets, here * rows, rows, block, seq_len)
    own_heads = heads // groups
    taps = lax.dynamic_slice_in_dim(filters, mine * own_heads, own_heads, axis=1)
    patterns = conv_patterns(taps.astype(jnp.bfloat16).astype(jnp.float32))

    tables = tables_of(patterns)
    out_near = lax.dynamic_slice_in_dim(out_weight, mine * half, half, axis=0)
    out_far = lax.dynamic_slice_in_dim(out_weight, (1 - mine) * half, half, axis=0)
    early, normed, mask, tables, out_near = lax.optimization_barrier(
        (early, normed, mask, tables, out_near)
    )
    one, two = flip(out_near, "ctx", 1), flip(out_near, "ctx", 2)
    states, gates, rim_fwd, rim_rev = early_sections(normed, early, tables, mask)
    rims = shifted(rim_fwd, "ctx", 1), shifted(rim_rev, "ctx", -1)
    one, two, states = lax.optimization_barrier((one, two, states))
    near = [out_near, one, two, flip(two, "ctx", 1)]
    far = [out_far, flip(one, "grp", 1), flip(two, "grp", 1)]
    late, far[2] = lax.optimization_barrier((late, far[2]))
    far.append(flip(near[3], "grp", 1))
    work = normed, late, states, gates, tables, mask, rims
    last_gate = last_gate_of(normed, late, 1)
    mixed_far = gated_sections(last_gate, states, gates, tables, mask, rims, 1)
    mixed_near = late_sections(*work, 0)
    from_y = flip(mixed_far, "grp", 1)
    from_xy = across(mixed_far, 2)
    from_x = flip(mixed_near, "ch", 2)
    near_pieces = [mixed_near, flip(mixed_near, "ch", 1), from_x, flip(from_x, "ch", 1)]
    far_pieces = [from_y, flip(from_y, "ch", 1), from_xy, flip(from_xy, "ch", 1)]
    return project_out(spots, near, far, near_pieces + far_pieces)


def solution(mesh):
    in_specs = (
        P(("grp", "ctx"), "ch"),
        P(("grp", "ctx"), "ch"),
        P(("grp", "ctx")),
        P(),
        P("grp"),
        P(None, "ch"),
        P(),
        P(None, "ctx", "ch"),
        P(None, "ch", None),
        P("ctx", "ch"),
    )
    out_specs = P(("grp", "ctx"), "ch")
    sizes = [mesh.shape[a] for a in ("grp", "ctx", "ch")]
    body = paired if sizes[0] == 2 and sizes[1] == sizes[2] == 4 else local
    return jax.shard_map(body, mesh=mesh, in_specs=in_specs, out_specs=out_specs, check_vma=False)
```

```python
import functools

import jax
import jax.numpy as jnp
from jax import lax
from jax.experimental import pallas as pl
from jax.experimental.pallas import tpu as pltpu
from jax.sharding import PartitionSpec as P

VMEM_LIMIT = 40 * 1024 * 1024
WIDE = 50 * 1024 * 1024
SMALL = pl.CostEstimate(flops=1, bytes_accessed=1, transcendentals=0)


def partner(block, axis, apart):
    count = lax.axis_size(axis)
    route = []
    for low in range(count):
        high = low | 1 << apart
        if high != low and high < count:
            route += [(low, high), (high, low)]
    return lax.ppermute(block, axis, route)


def shifted(value, axis, by):
    count = lax.axis_size(axis)
    pairs = [(i, i + by) for i in range(count) if 0 <= i + by < count]
    return lax.ppermute(value, axis, pairs)


def doc_of(positions, offsets, seq_len):
    count = jnp.sum((offsets[None, :] <= positions[:, None]).astype(jnp.int32), axis=1) - 1
    inside = (positions >= 0) & (positions < seq_len)
    return jnp.where(inside, count, -1)


def toeplitz(taps):
    heads, block = taps.shape
    pattern = jnp.concatenate(
        [jnp.zeros((heads, 1), taps.dtype), taps[:, ::-1], jnp.zeros((heads, block), taps.dtype)],
        axis=1,
    )
    repeated = jnp.tile(pattern, (1, block))
    return repeated[:, : block * 2 * block].reshape(heads, block, 2 * block)


def rms_norm(values, gain):
    floats = values.astype(jnp.float32)
    scale = lax.rsqrt(jnp.mean(floats * floats, axis=-1, keepdims=True) + 1e-05)
    return (floats * scale * gain).astype(jnp.bfloat16)


def blockwise_conv(conv_in, rim, taps, ext_docs):
    rows, width = conv_in.shape
    heads, block = taps.shape
    head_dim = width // heads
    blocks = rows // block
    extended = jnp.concatenate([rim, conv_in], axis=0)
    target_docs = ext_docs[block:].reshape(blocks, block)
    window = jnp.concatenate(
        [
            extended[:rows].reshape(blocks, block, width),
            extended[block:].reshape(blocks, block, width),
        ],
        axis=1,
    )
    window = window.reshape(blocks, 2 * block, heads, head_dim)
    window_docs = jnp.concatenate(
        [ext_docs[:rows].reshape(blocks, block), ext_docs[block:].reshape(blocks, block)], axis=1
    )
    mask = (target_docs[:, :, None] == window_docs[:, None, :]).astype(jnp.bfloat16)
    kernel = toeplitz(taps)[None] * mask[:, None]
    result = jnp.einsum("nhts,nshd->nthd", kernel, window, preferred_element_type=jnp.float32)
    return result.reshape(rows, width)


def local(
    fwd_hidden,
    rev_hidden,
    bases,
    complement,
    offsets,
    base_embed,
    norm_gain,
    in_weight,
    filters,
    out_weight,
):
    rows, width_local = fwd_hidden.shape
    ctx_count = lax.axis_size("ctx")
    here = lax.axis_index("ctx")
    seq_len = rows * ctx_count
    letters = base_embed.shape[0]
    alphabet = jnp.arange(letters, dtype=jnp.int32)
    onehot = (bases[:, None] == alphabet[None, :]).astype(jnp.bfloat16)
    swap_table = (complement[:, None] == alphabet[None, :]).astype(jnp.bfloat16)
    onehot_rev = jnp.dot(onehot, swap_table, preferred_element_type=jnp.float32).astype(
        jnp.bfloat16
    )
    embed_fwd = jnp.dot(onehot, base_embed, preferred_element_type=jnp.float32)
    embed_rev = jnp.dot(onehot_rev, base_embed, preferred_element_type=jnp.float32)
    fwd_input = (fwd_hidden.astype(jnp.float32) + embed_fwd).astype(jnp.bfloat16)
    rev_input = (rev_hidden.astype(jnp.float32) + embed_rev).astype(jnp.bfloat16)
    levels = ctx_count.bit_length() - 1
    for level in range(levels):
        rev_input = partner(rev_input, "ctx", level)
    rev_input = rev_input[::-1]
    full_fwd, full_rev = (
        lax.all_gather(fwd_input, "ch", axis=1, tiled=True),
        lax.all_gather(rev_input, "ch", axis=1, tiled=True),
    )
    normed_fwd = rms_norm(full_fwd, norm_gain)
    normed_rev = rms_norm(full_rev, norm_gain)
    piece = lax.all_gather(in_weight, "ctx", axis=1, tiled=True)
    add_fwd = jnp.einsum("rd,bdc->brc", normed_fwd, piece, preferred_element_type=jnp.float32)
    add_rev = jnp.einsum("rd,bdc->brc", normed_rev, piece, preferred_element_type=jnp.float32)
    taps_all = filters.astype(jnp.bfloat16)
    block = filters.shape[-1]
    before = here * rows - block + jnp.arange(rows + block, dtype=jnp.int32)
    docs_fwd = doc_of(before, offsets, seq_len)
    docs_rev = doc_of(seq_len - 1 - before, offsets, seq_len)
    state_fwd = add_fwd[0]
    state_rev = add_rev[0]
    for section in range(filters.shape[0]):
        in_fwd = state_fwd.astype(jnp.bfloat16)
        in_rev = state_rev.astype(jnp.bfloat16)
        rim_fwd, rim_rev = shifted((in_fwd[-block:], in_rev[-block:]), "ctx", 1)
        conv_rev = blockwise_conv(in_rev, rim_rev, taps_all[section], docs_rev)
        conv_fwd = blockwise_conv(in_fwd, rim_fwd, taps_all[section], docs_fwd)
        state_fwd = add_fwd[section + 1] * conv_fwd
        state_rev = add_rev[section + 1] * conv_rev
    mixed_fwd = state_fwd.astype(jnp.bfloat16)
    mixed_rev = state_rev.astype(jnp.bfloat16)
    for level in range(levels):
        mixed_rev = partner(mixed_rev, "ctx", level)
    mixed_rev = mixed_rev[::-1]
    mixed_sum = (mixed_fwd.astype(jnp.float32) + mixed_rev.astype(jnp.float32)).astype(jnp.bfloat16)
    whole_sum = lax.all_gather(mixed_sum, "ch", axis=1, tiled=True)
    total = jnp.dot(
        whole_sum,
        lax.all_gather(out_weight, "ctx", axis=0, tiled=True),
        preferred_element_type=jnp.float32,
    )
    return total.astype(jnp.bfloat16)


def flip(block, axis, bit):
    count = lax.axis_size(axis)
    return lax.ppermute(block, axis, [(i, i ^ bit) for i in range(count)])


def across(block, bit):
    groups, count = lax.axis_size("grp"), lax.axis_size("ch")
    pairs = [
        (g * count + k, (g ^ 1) * count + (k ^ bit)) for g in range(groups) for k in range(count)
    ]
    return lax.ppermute(block, ("grp", "ch"), pairs)


def params(*semantics, limit=None):
    return pltpu.CompilerParams(
        dimension_semantics=semantics, vmem_limit_bytes=limit or VMEM_LIMIT
    )


def gathered(block):
    two = flip(block, "ctx", 2)
    return [block, flip(block, "ctx", 1), two, flip(two, "ctx", 1)]


def after(value, *others):
    return lax.optimization_barrier((value,) + others)[0]


def norm_kernel(layout, place, gain, *refs):
    out = refs[-1]
    for s, strand in enumerate(layout):
        for g, group in enumerate(strand):
            blocks = [refs[n][...] if at is None else refs[n][at] for n, at in group]
            width = blocks[0].shape[-1]
            model = width * len(blocks)
            floats = [p.astype(jnp.float32) for p in blocks]
            total = sum(f * f for f in floats)
            scale = lax.rsqrt(jnp.sum(total, axis=-1, keepdims=True) / model + 1e-05)
            for j, f in enumerate(floats):
                lanes = pl.ds(pl.multiple_of((place[0] ^ j) * width, width), width)
                out[s, g, :, lanes] = (f * scale * gain[:, lanes]).astype(jnp.bfloat16)


def norm_all(place, gain, layout, arrays):
    strands, groups, parts = len(layout), len(layout[0]), len(layout[0][0])
    rows, width = arrays[0].shape[-2:]
    tile = 128

    def spec(array):
        if array.ndim == 2:
            return pl.BlockSpec((tile, width), lambda i, p: (i, 0))
        return pl.BlockSpec((strands, tile, width), lambda i, p: (0, i, 0))

    shape = (strands, groups, rows, width * parts)
    return pl.pallas_call(
        functools.partial(norm_kernel, layout),
        grid_spec=pltpu.PrefetchScalarGridSpec(
            num_scalar_prefetch=1,
            grid=(rows // tile,),
            in_specs=[pl.BlockSpec((1, width * parts), lambda i, p: (0, 0))]
            + [spec(v) for v in arrays],
            out_specs=pl.BlockSpec(
                (strands, groups, tile, width * parts), lambda i, p: (0, 0, i, 0)
            ),
        ),
        out_shape=jax.ShapeDtypeStruct(shape, jnp.bfloat16),
        compiler_params=params("arbitrary"),
        cost_estimate=SMALL,
        name="norm",
    )(place, gain.reshape(1, -1), *arrays)


CUTS = 2


def fetch(normed, weight, count, order, held, kept, x_sems, w_sems):
    depth = weight.shape[2]
    for b in range(count):
        for z in range(weight.shape[0]):
            span = pl.ds(z * depth, depth)
            pltpu.make_async_copy(
                weight.at[z, b], kept.at[b, span], w_sems.at[b, z]
            ).start()
    groups, rows = normed.shape[1:3]
    part = rows // CUTS
    for s, g in order:
        at = s * groups + g
        for c in range(CUTS):
            span = pl.ds(c * part, part)
            pltpu.make_async_copy(
                normed.at[s, g, span], held.at[at, span], x_sems.at[at, c]
            ).start()


def wait_weight(weight, count, kept, w_sems):
    depth = weight.shape[2]
    for b in range(count):
        for z in range(weight.shape[0]):
            span = pl.ds(z * depth, depth)
            pltpu.make_async_copy(weight.at[z, 0], kept.at[b, span], w_sems.at[b, z]).wait()


def wait_rows(normed, at, held, x_sems):
    part = normed.shape[2] // CUTS
    for c in range(CUTS):
        span = pl.ds(c * part, part)
        pltpu.make_async_copy(normed.at[0, 0, span], held.at[at, span], x_sems.at[at, c]).wait()


def product(value, weight):
    return jnp.dot(value[...], weight[...], preferred_element_type=jnp.float32)


def fetch_scratch(normed, weight, count):
    strands, groups, rows, model = normed.shape
    blocks, _, depth, width = weight.shape
    return [
        pltpu.VMEM((strands * groups, rows, model), jnp.bfloat16),
        pltpu.VMEM((count, blocks * depth, width), jnp.bfloat16),
        pltpu.SemaphoreType.DMA((strands * groups, CUTS)),
        pltpu.SemaphoreType.DMA((count, blocks)),
    ]


def toeplitz_of(pattern, block):
    width = pattern.shape[-1]
    spread = jnp.broadcast_to(pattern, (block, width))
    return pltpu.roll(spread, 0, 1, stride=1, stride_axis=0).astype(jnp.bfloat16)


def tables_kernel(patterns, tables):
    block = tables.shape[-2]
    for k in range(tables.shape[0]):
        for h in range(tables.shape[2]):
            tables[k, 0, h] = toeplitz_of(patterns[k, 0, h], block)


def tables_of(patterns):
    sections, strands, heads, _, width = patterns.shape
    block = width // 2
    return pl.pallas_call(
        tables_kernel,
        grid=(strands,),
        in_specs=[pl.BlockSpec((sections, 1, heads, 1, width), lambda s: (0, s, 0, 0, 0))],
        out_specs=pl.BlockSpec((sections, 1, heads, block, width), lambda s: (0, s, 0, 0, 0)),
        out_shape=jax.ShapeDtypeStruct((sections, strands, heads, block, width), jnp.bfloat16),
        compiler_params=params("arbitrary"),
        cost_estimate=SMALL,
        name="tables",
    )(patterns)


def gated_block(k, s, n, blocks, window, table, mask, gate, gate_at=None):
    block = table.shape[-2]
    place = jnp.where(s == 0, n, blocks - 1 - n)
    at = pl.multiple_of(place * block, block)
    heads = table.shape[2]
    head = gate.shape[-1] // heads
    gate_at = at if gate_at is None else gate_at
    out = []
    for h in range(heads):
        lanes = slice(h * head, (h + 1) * head)
        conv = jnp.dot(
            table[k, 0, h] * mask[0, 0, place],
            window[pl.ds(at, 2 * block), lanes],
            preferred_element_type=jnp.float32,
        )
        out.append((gate[pl.ds(gate_at, block), lanes] * conv).astype(jnp.bfloat16))
    return at, jnp.concatenate(out, axis=-1)


def shifted_at(at, s, block):
    return pl.multiple_of(at + jnp.where(s == 0, block, 0), block)


def early_kernel(normed, weight, table, mask, *refs):
    s, g = pl.program_id(0), pl.program_id(1)
    states, gates_out, rim_fwd, rim_rev = refs[:4]
    held, kept, x_sems, w_sems, *extended = refs[4:8] + refs[8:10]
    gates = refs[10:]
    groups, rows = normed.shape[1:3]
    block = table.shape[-2]
    blocks = rows // block

    @pl.when((s == 0) & (g == 0))
    def _():
        order = [(i, j) for i in range(normed.shape[0]) for j in range(groups)]
        fetch(normed, weight, 3, order, held, kept, x_sems, w_sems)
        wait_weight(weight, 3, kept, w_sems)

    def row_of(n):
        return pl.multiple_of(jnp.where(s == 0, n, blocks - 1 - n) * block, block)

    def keep_rim(k, value):
        @pl.when(s == 0)
        def _():
            rim_fwd[k, g] = value

        @pl.when(s == 1)
        def _():
            rim_rev[k, g] = value

    at = s * groups + g
    wait_rows(normed, at, held, x_sems)
    extended[0][pl.ds(shifted_at(0, s, block), rows)] = product(
        held.at[at], kept.at[0]
    ).astype(jnp.bfloat16)
    states[0, 0, 0] = extended[0][pl.ds(shifted_at(row_of(0), s, block), block)]
    keep_rim(0, extended[0][pl.ds(shifted_at(row_of(blocks - 1), s, block), block)])
    for k in range(2):
        gates[k][...] = product(held.at[at], kept.at[k + 1])
    gates_out[0, 0, 0] = gates[0][pl.ds(row_of(0), block)]
    for n in range(2):
        gates_out[0, 0, 1 + n] = gates[1][pl.ds(row_of(n), block)]
    for n in range(1, blocks):
        row, value = gated_block(0, s, n, blocks, extended[0], table, mask, gates[0])
        extended[1][pl.ds(shifted_at(row, s, block), block)] = value
        if n == 1:
            states[0, 0, 1] = value
    keep_rim(1, value)
    for n in range(2, blocks):
        row, value = gated_block(1, s, n, blocks, extended[1], table, mask, gates[1])
        states[0, 0, n] = value
    keep_rim(2, value)


def early_sections(normed, weight, tables, mask):
    strands, groups, rows, _ = normed.shape
    width = weight.shape[-1]
    sections, _, heads, block, _ = tables.shape
    blocks = rows // block
    rim = jax.ShapeDtypeStruct((sections, groups, block, width), jnp.bfloat16)
    rim_spec = pl.BlockSpec(rim.shape, lambda s, g: (0, 0, 0, 0))
    return pl.pallas_call(
        early_kernel,
        grid=(strands, groups),
        in_specs=[pl.BlockSpec(memory_space=pltpu.HBM)] * 2
        + [
            pl.BlockSpec((sections, 1, heads, block, 2 * block), lambda s, g: (0, s, 0, 0, 0)),
            pl.BlockSpec((1, 1, blocks, block, 2 * block), lambda s, g: (s, g, 0, 0, 0)),
        ],
        out_specs=[
            pl.BlockSpec((1, 1, blocks, block, width), lambda s, g: (s, g, 0, 0, 0)),
            pl.BlockSpec((1, 1, 3, block, width), lambda s, g: (s, g, 0, 0, 0)),
            rim_spec,
            rim_spec,
        ],
        out_shape=[
            jax.ShapeDtypeStruct((strands, groups, blocks, block, width), jnp.bfloat16),
            jax.ShapeDtypeStruct((strands, groups, 3, block, width), jnp.float32),
            rim,
            rim,
        ],
        scratch_shapes=fetch_scratch(normed, weight, 3)
        + [pltpu.VMEM((rows + block, width), jnp.bfloat16)] * 2
        + [pltpu.VMEM((rows, width), jnp.float32)] * 2,
        compiler_params=params("arbitrary", "arbitrary", limit=WIDE),
        cost_estimate=SMALL,
        name="early_sections",
    )(normed, weight, tables, mask)


def late_kernel(g, normed, weight, states, gates, table, mask, *refs):
    rims, out = refs[:2], refs[2]
    held, kept, x_sems, w_sems, last_gate, *extended = refs[3:]
    s = pl.program_id(0)
    groups, rows = normed.shape[1:3]
    block = table.shape[-2]
    blocks = rows // block

    @pl.when(s == 0)
    def _():
        order = [(i, g) for i in range(normed.shape[0])]
        fetch(normed, weight, 1, order, held, kept, x_sems, w_sems)

    def put(k, n, value):
        at = jnp.where(s == 0, n, blocks - 1 - n) * block
        extended[k][pl.ds(shifted_at(at, s, block), block)] = value

    for k in range(3):

        @pl.when(s == 0)
        def _():
            extended[k][:block] = rims[0][k, 0]

        @pl.when(s == 1)
        def _():
            extended[k][rows:] = rims[1][k, 0]

    put(0, 0, states[0, 0, 0])
    put(1, 1, states[0, 0, 1])
    for n in range(2, blocks):
        put(2, n, states[0, 0, n])
    for k in range(2):
        for n in range(k + 1):
            gate = gates.at[0, 0, k + n]
            _, value = gated_block(k, s, n, blocks, extended[k], table, mask, gate, 0)
            put(k + 1, n, value)

    @pl.when(s == 0)
    def _():
        wait_weight(weight, 1, kept, w_sems)

    at = s * groups + g
    wait_rows(normed, at, held, x_sems)
    last_gate[...] = product(held.at[at], kept.at[0])
    for n in range(blocks):
        row, value = gated_block(2, s, n, blocks, extended[2], table, mask, last_gate)
        span = pl.ds(row, block)
        before = jnp.where(s == 0, 0.0, out[span].astype(jnp.float32))
        out[span] = (before + value.astype(jnp.float32)).astype(jnp.bfloat16)


def late_sections(normed, weight, states, gates, tables, mask, rims, g):
    strands, groups, rows, _ = normed.shape
    blocks, block, width = states.shape[2:]
    sections, _, heads = tables.shape[:3]
    return pl.pallas_call(
        functools.partial(late_kernel, g),
        grid=(strands,),
        in_specs=[pl.BlockSpec(memory_space=pltpu.HBM)] * 2
        + [
            pl.BlockSpec((1, 1, blocks, block, width), lambda s: (s, g, 0, 0, 0)),
            pl.BlockSpec((1, 1, 3, block, width), lambda s: (s, g, 0, 0, 0)),
            pl.BlockSpec((sections, 1, heads, block, 2 * block), lambda s: (0, s, 0, 0, 0)),
            pl.BlockSpec((1, 1, blocks, block, 2 * block), lambda s: (s, g, 0, 0, 0)),
        ]
        + [pl.BlockSpec((sections, 1, block, width), lambda s: (0, g, 0, 0)) for _ in rims],
        out_specs=pl.BlockSpec((rows, width), lambda s: (0, 0)),
        out_shape=jax.ShapeDtypeStruct((rows, width), jnp.bfloat16),
        scratch_shapes=fetch_scratch(normed, weight, 1)
        + [pltpu.VMEM((rows, width), jnp.float32)]
        + [pltpu.VMEM((rows + block, width), jnp.bfloat16)] * 3,
        compiler_params=params("arbitrary", limit=WIDE),
        cost_estimate=SMALL,
        name="late_sections",
    )(normed, weight, states, gates, tables, mask, *rims)


def last_gate_kernel(g, normed, weight, out, held, kept, x_sems, w_sems):
    s = pl.program_id(0)

    @pl.when(s == 0)
    def _():
        order = [(i, g) for i in range(normed.shape[0])]
        fetch(normed, weight, 1, order, held, kept, x_sems, w_sems)
        wait_weight(weight, 1, kept, w_sems)

    at = s * normed.shape[1] + g
    wait_rows(normed, at, held, x_sems)
    out[0] = product(held.at[at], kept.at[0])


def last_gate_of(normed, weight, g):
    strands, _, rows, _ = normed.shape
    width = weight.shape[-1]
    return pl.pallas_call(
        functools.partial(last_gate_kernel, g),
        grid=(strands,),
        in_specs=[pl.BlockSpec(memory_space=pltpu.HBM)] * 2,
        out_specs=pl.BlockSpec((1, rows, width), lambda s: (s, 0, 0)),
        out_shape=jax.ShapeDtypeStruct((strands, rows, width), jnp.float32),
        scratch_shapes=fetch_scratch(normed, weight, 1),
        compiler_params=params("arbitrary", limit=WIDE),
        cost_estimate=SMALL,
        name="last_gate",
    )(normed, weight)


def gated_kernel(last_gate, states, gates, table, mask, *refs):
    rims, out = refs[:2], refs[2]
    extended = refs[3:]
    s = pl.program_id(0)
    block = table.shape[-2]
    rows = out.shape[0]
    blocks = rows // block

    def put(k, n, value):
        at = jnp.where(s == 0, n, blocks - 1 - n) * block
        extended[k][pl.ds(shifted_at(at, s, block), block)] = value

    for k in range(3):

        @pl.when(s == 0)
        def _():
            extended[k][:block] = rims[0][k, 0]

        @pl.when(s == 1)
        def _():
            extended[k][rows:] = rims[1][k, 0]

    put(0, 0, states[0, 0, 0])
    put(1, 1, states[0, 0, 1])
    for n in range(2, blocks):
        put(2, n, states[0, 0, n])
    for k in range(2):
        for n in range(k + 1):
            gate = gates.at[0, 0, k + n]
            _, value = gated_block(k, s, n, blocks, extended[k], table, mask, gate, 0)
            put(k + 1, n, value)

    for n in range(blocks):
        row, value = gated_block(2, s, n, blocks, extended[2], table, mask, last_gate.at[0])
        span = pl.ds(row, block)
        before = jnp.where(s == 0, 0.0, out[span].astype(jnp.float32))
        out[span] = (before + value.astype(jnp.float32)).astype(jnp.bfloat16)


def gated_sections(last_gate, states, gates, tables, mask, rims, g):
    strands, rows, _ = last_gate.shape
    blocks, block, width = states.shape[2:]
    sections, _, heads = tables.shape[:3]
    return pl.pallas_call(
        gated_kernel,
        grid=(strands,),
        in_specs=[pl.BlockSpec((1, rows, width), lambda s: (s, 0, 0))]
        + [
            pl.BlockSpec((1, 1, blocks, block, width), lambda s: (s, g, 0, 0, 0)),
            pl.BlockSpec((1, 1, 3, block, width), lambda s: (s, g, 0, 0, 0)),
            pl.BlockSpec((sections, 1, heads, block, 2 * block), lambda s: (0, s, 0, 0, 0)),
            pl.BlockSpec((1, 1, blocks, block, 2 * block), lambda s: (s, g, 0, 0, 0)),
        ]
        + [pl.BlockSpec((sections, 1, block, width), lambda s: (0, g, 0, 0)) for _ in rims],
        out_specs=pl.BlockSpec((rows, width), lambda s: (0, 0)),
        out_shape=jax.ShapeDtypeStruct((rows, width), jnp.bfloat16),
        scratch_shapes=[pltpu.VMEM((rows + block, width), jnp.bfloat16)] * 3,
        compiler_params=params("arbitrary", limit=WIDE),
        cost_estimate=SMALL,
        name="gated_sections",
    )(last_gate, states, gates, tables, mask, *rims)


def out_kernel(parts, spots, *refs):
    weights, pieces = refs[: 2 * parts], refs[2 * parts : -2]
    out, held = refs[-2:]

    @pl.when(pl.program_id(0) == 0)
    def _():
        for half in range(2):
            for i in range(parts):
                held[half, spots[1] ^ i] = weights[half * parts + i][...]

    total = None
    for half in range(2):
        for j in range(parts):
            piece = pieces[half * parts + j]
            term = jnp.dot(
                piece[...], held[half, spots[0] ^ j], preferred_element_type=jnp.float32
            )
            total = term if total is None else total + term
    out[...] = total.astype(jnp.bfloat16)


def project_out(spots, near, far, pieces):
    parts = len(near)
    rows, depth = pieces[0].shape
    width = near[0].shape[-1]
    tile = rows
    return pl.pallas_call(
        functools.partial(out_kernel, parts),
        grid_spec=pltpu.PrefetchScalarGridSpec(
            num_scalar_prefetch=1,
            grid=(rows // tile,),
            in_specs=[pl.BlockSpec(w.shape, lambda i, p: (0, 0)) for w in near + far]
            + [pl.BlockSpec((tile, depth), lambda i, p: (i, 0)) for _ in pieces],
            out_specs=pl.BlockSpec((tile, width), lambda i, p: (i, 0)),
            scratch_shapes=[pltpu.VMEM((2, parts, depth, width), jnp.bfloat16)],
        ),
        out_shape=jax.ShapeDtypeStruct((rows, width), jnp.bfloat16),
        compiler_params=params("arbitrary"),
        cost_estimate=SMALL,
        name="out",
    )(spots, *near, *far, *pieces)


def conv_patterns(taps):
    zero = jnp.zeros_like(taps)
    forward = jnp.concatenate([zero[..., :1], taps[..., ::-1], zero[..., 1:]], axis=-1)
    reverse = jnp.concatenate([taps, zero], axis=-1)
    return jnp.stack([forward, reverse], axis=1)[:, :, :, None, :]


def doc_masks(offsets, start, rows, block, seq_len):
    positions = start - block + jnp.arange(rows + 2 * block, dtype=jnp.int32)
    docs = jax.vmap(lambda o: doc_of(positions, o, seq_len))(offsets)
    groups, blocks = offsets.shape[0], rows // block
    tiles = docs.reshape(groups, blocks + 2, block)
    target = tiles[:, 1:-1]
    before = jnp.concatenate([tiles[:, :-2], target], axis=-1)
    after = jnp.concatenate([target, tiles[:, 2:]], axis=-1)
    window = jnp.stack([before, after])
    return (target[None, :, :, :, None] == window[:, :, :, None, :]).astype(jnp.bfloat16)


def paired(
    fwd_hidden,
    rev_hidden,
    bases,
    complement,
    offsets,
    base_embed,
    norm_gain,
    in_weight,
    filters,
    out_weight,
):
    rows, width = fwd_hidden.shape
    groups, ctx_count, parts = (lax.axis_size(a) for a in ("grp", "ctx", "ch"))
    mine, here, place = (lax.axis_index(a) for a in ("grp", "ctx", "ch"))
    sections, heads, block = filters.shape
    seq_len = rows * ctx_count
    half = width // groups

    columns = lax.dynamic_slice_in_dim(in_weight, mine * half, half, axis=2)
    early = lax.all_gather(columns[:sections], "ctx", axis=0)

    letters = base_embed.shape[0]
    alphabet = jnp.arange(letters, dtype=jnp.int32)
    onehot = (bases[:, None] == alphabet[None, :]).astype(jnp.bfloat16)
    swap_table = (complement[:, None] == alphabet[None, :]).astype(jnp.bfloat16)
    swapped = jnp.dot(swap_table, base_embed, preferred_element_type=jnp.float32)
    inputs = []
    for hidden, table in ((fwd_hidden, base_embed), (rev_hidden, swapped.astype(jnp.bfloat16))):
        embed = jnp.dot(onehot, table, preferred_element_type=jnp.float32)
        inputs.append((hidden.astype(jnp.float32) + embed).astype(jnp.bfloat16))
    own = jnp.stack(inputs)
    x = flip(own, "ch", 2)
    y = flip(own, "grp", 1)
    core = flip(own, "ch", 1)
    x, y, core = lax.optimization_barrier((x, y, core))
    xy = [flip(x[0], "grp", 1), flip(y[1], "ch", 2)]
    arrays = [own, core, x, flip(x, "ch", 1), y, flip(y, "ch", 1)]
    arrays += [xy[0], flip(xy[0], "ch", 1), xy[1], flip(xy[1], "ch", 1)]
    layout = [
        [
            [(n, s) for n in range(1, 5)],
            [(5, s), (6, s), (7 + 2 * s, None), (8 + 2 * s, None)],
        ]
        for s in range(2)
    ]
    layout = [[[(n - 1, at) for n, at in group] for group in strand] for strand in layout]
    spots = jnp.stack([place, here]).astype(jnp.int32)
    normed = norm_all(spots, norm_gain, layout, arrays)
    late = lax.all_gather(after(columns[sections:], x), "ctx", axis=0)

    both_offsets = jnp.stack([offsets, flip(offsets, "grp", 1)])
    mask = doc_masks(both_offsets, here * rows, rows, block, seq_len)
    own_heads = heads // groups
    taps = lax.dynamic_slice_in_dim(filters, mine * own_heads, own_heads, axis=1)
    patterns = conv_patterns(taps.astype(jnp.bfloat16).astype(jnp.float32))

    tables = tables_of(patterns)
    out_near = lax.dynamic_slice_in_dim(out_weight, mine * half, half, axis=0)
    out_far = lax.dynamic_slice_in_dim(out_weight, (1 - mine) * half, half, axis=0)
    early, normed, mask, tables, out_near = lax.optimization_barrier(
        (early, normed, mask, tables, out_near)
    )
    one, two = flip(out_near, "ctx", 1), flip(out_near, "ctx", 2)
    states, gates, rim_fwd, rim_rev = early_sections(normed, early, tables, mask)
    rims = shifted(rim_fwd, "ctx", 1), shifted(rim_rev, "ctx", -1)
    one, two, states = lax.optimization_barrier((one, two, states))
    near = [out_near, one, two, flip(two, "ctx", 1)]
    far = [out_far, flip(one, "grp", 1), flip(two, "grp", 1)]
    late, far[2] = lax.optimization_barrier((late, far[2]))
    far.append(flip(near[3], "grp", 1))
    work = normed, late, states, gates, tables, mask, rims
    last_gate = last_gate_of(normed, late, 1)
    mixed_far = gated_sections(last_gate, states, gates, tables, mask, rims, 1)
    mixed_near = late_sections(*work, 0)
    from_y = flip(mixed_far, "grp", 1)
    from_xy = across(mixed_far, 2)
    from_x = flip(mixed_near, "ch", 2)
    near_pieces = [mixed_near, flip(mixed_near, "ch", 1), from_x, flip(from_x, "ch", 1)]
    far_pieces = [from_y, flip(from_y, "ch", 1), from_xy, flip(from_xy, "ch", 1)]
    return project_out(spots, near, far, near_pieces + far_pieces)


def solution(mesh):
    in_specs = (
        P(("grp", "ctx"), "ch"),
        P(("grp", "ctx"), "ch"),
        P(("grp", "ctx")),
        P(),
        P("grp"),
        P(None, "ch"),
        P(),
        P(None, "ctx", "ch"),
        P(None, "ch", None),
        P("ctx", "ch"),
    )
    out_specs = P(("grp", "ctx"), "ch")
    sizes = [mesh.shape[a] for a in ("grp", "ctx", "ch")]
    body = paired if sizes[0] == 2 and sizes[1] == sizes[2] == 4 else local
    return jax.shard_map(body, mesh=mesh, in_specs=in_specs, out_specs=out_specs, check_vma=False)
```
